32 devices in a mesh: inner: 8 (over z, y), cols: 4 (over x, core).
Axes of the slice: x: 2, y: 2, z: 4, core: 2. Of those that a mesh axis runs over, the one named last changes fastest.
Arguments:
- left_u: bfloat16 [64, 512, 128], P(('inner', 'cols')), may hold values from -6 to 6
- left_v: bfloat16 [64, 512, 128], P(('inner', 'cols')), may hold values from -0.0234375 to 0.0234375
- right_u: bfloat16 [16, 64, 512, 128], P('cols', 'inner'), may hold values from -6 to 6
- right_v: bfloat16 [16, 64, 512, 128], P('cols', 'inner'), may hold values from -0.1875 to 0.1875
- sketch: bfloat16 [16, 512, 128], P('cols'), may hold values from -0.25 to 0.25
- tile_index: int32 [16, 64], P('cols', 'inner'), may hold values from 0 to 63, as said below
- slot_mask: int32 [16, 64], P('cols', 'inner'), may hold values from 0 to 1, as said below
Outputs:
- basis: float32 [16, 512, 128], P('cols', 'inner')
- coeff: float32 [16, 512, 128], P('cols', 'inner')
The draws below stay inside these ranges and needn't reach their ends.
Inputs may be any that keep to these rules, and one draw needn't show every extreme that they name: `tile_index`: slot s of an output tile belongs to inner group g = s // 8 and names a left tile of that group, g * 8 to g * 8 + 7; the tiles named by one output tile's slots of one group are distinct. `slot_mask`: in each output tile and inner group the live slots come first and there is at least one; in every output tile some group has all 8 slots live, and the others at most 4.
All inputs are finite; a program needn't handle non-finite values.
Results may differ from the reference program's by a relative error of at most 0.0045.
Values may be sent and summed in bfloat16 or wider, within the bound.
A program may use at most 64 MiB of HBM per device.

```python
import math
import jax
import jax.numpy as jnp
from jax import lax

NB = 512
R = 128
SLOTS = 8
OUT = 16
LISTS = 64
TILES = 64


def draw_tile_index(key, part):
    groups = LISTS // SLOTS
    keys = jax.random.split(jax.random.fold_in(key, 11), OUT * groups)
    orders = jax.vmap(lambda sub_key: jax.random.permutation(sub_key, SLOTS))(keys)
    orders = orders.reshape(OUT, groups, SLOTS).astype(jnp.int32)
    offsets = (jnp.arange(groups, dtype=jnp.int32) * SLOTS)[None, :, None]
    return (orders + offsets).reshape(OUT, LISTS).astype(jnp.int32)


def draw_slot_mask(key, part):
    groups = LISTS // SLOTS
    first_key, second_key = jax.random.split(jax.random.fold_in(key, 23))
    counts = jax.random.randint(first_key, (OUT, groups), 1, SLOTS // 2 + 1)
    busiest = jax.random.randint(second_key, (OUT,), 0, groups)
    counts = jnp.where(jnp.arange(groups)[None, :] == busiest[:, None], SLOTS, counts)
    filled = jnp.arange(SLOTS)[None, None, :] < counts[:, :, None]
    return filled.astype(jnp.int32).reshape(OUT, LISTS)


def level_of(stream_key, extent, shards, smallest, high):
    gain, own = 1.0, jax.random.fold_in(stream_key, 6)
    for position, blocks in shards:
        heights = jnp.exp(jax.random.uniform(jax.random.fold_in(own, position), (blocks,), jnp.float32, smallest / len(shards), high / len(shards)))
        gain = gain * jnp.repeat(heights, extent[position] // blocks).reshape([-1 if axis == position else 1 for axis in range(len(extent))])
    return gain


def gaussian(stream_key, extent, width, reach, cuts=(), kind=jnp.bfloat16):
    array = jax.random.normal(stream_key, extent, jnp.float32) * width
    if len(cuts) > 0:
        array = level_of(stream_key, extent, cuts, -0.22, 0.18) * array
    return jnp.clip(array, min=-reach, max=reach).astype(kind)


def setup_inputs(seed: int = 0) -> dict:
    key_list = jax.random.split(jax.random.key(seed), 8)
    return {
        "left_u": gaussian(key_list[0], (TILES, NB, R), 1.0, 6.0, ((0, 32),)),
        "left_v": gaussian(key_list[1], (TILES, NB, R), (R * NB) ** -0.5, 0.0234375, ((0, 32),)),
        "right_u": gaussian(key_list[2], (OUT, LISTS, NB, R), 1.0, 6.0, ((0, 4), (1, 8))),
        "right_v": gaussian(key_list[3], (OUT, LISTS, NB, R), (R * LISTS // SLOTS) ** -0.5, 0.1875, ((0, 4), (1, 8))),
        "sketch": gaussian(key_list[4], (OUT, NB, R), NB ** -0.5, 0.25, ((0, 4),)),
        "tile_index": draw_tile_index(jax.random.fold_in(key_list[7], 71), 0),
        "slot_mask": draw_slot_mask(jax.random.fold_in(key_list[7], 71), 0),
    }


HIGH = lax.Precision.HIGHEST

def one_tile(left_u, left_v, right_ub, right_vb, sketch_j, index_j, mask_j):
    live_mask = mask_j.astype(jnp.float32)
    tile_u = jnp.take(left_u, index_j, axis=0).astype(jnp.float32)
    tile_v = jnp.take(left_v, index_j, axis=0).astype(jnp.float32)
    right_uf = right_ub.astype(jnp.float32)
    right_vf = right_vb.astype(jnp.float32)
    pairing = jnp.einsum('sna,snb->sab', tile_v, right_uf, precision=HIGH)
    probe = jnp.einsum('snb,nt->sbt', right_vf, sketch_j.astype(jnp.float32), precision=HIGH)
    mixing = (live_mask[:, None, None] * jnp.einsum('sab,sbt->sat', pairing, probe, precision=HIGH)).astype(jnp.bfloat16)
    sketched = jnp.einsum('sna,sat->nt', tile_u, mixing.astype(jnp.float32), precision=HIGH)
    gram_mat = jnp.dot(sketched.T, sketched, precision=HIGH)
    factor = jnp.linalg.cholesky(gram_mat)
    ortho = jax.scipy.linalg.solve_triangular(factor, sketched.T, lower=True).T
    basis = ortho * math.sqrt(NB)
    ortho_b = ortho.astype(jnp.bfloat16)
    projected = jnp.einsum('sna,nt->sat', tile_u, ortho_b.astype(jnp.float32), precision=HIGH)
    backward = (live_mask[:, None, None] * jnp.einsum('sab,sat->sbt', pairing, projected, precision=HIGH)).astype(jnp.bfloat16)
    coeff = jnp.einsum('snb,sbt->nt', right_vf, backward.astype(jnp.float32), precision=HIGH)
    return (basis, coeff)

def reference(left_u, left_v, right_u, right_v, sketch, tile_index, slot_mask):

    def per_tile(items):
        return one_tile(left_u, left_v, items[0], items[1], items[2], items[3], items[4])
    basis, coeff = lax.map(per_tile, (right_u, right_v, sketch, tile_index, slot_mask))
    return (basis, coeff)
```

```python
import functools
import math

import jax
import jax.numpy as jnp
from jax import lax
from jax.experimental import pallas as pl
from jax.experimental.pallas import tpu as pltpu
from jax.sharding import PartitionSpec as P

MESH = pl.DeviceIdType.MESH
F32 = jnp.float32
BF16 = jnp.bfloat16
NN = (((1,), (0,)), ((), ()))
NT = (((1,), (1,)), ((), ()))
TN = (((0,), (0,)), ((), ()))


def mm(a, b, dims):
    return lax.dot_general(a, b, dims, preferred_element_type=F32)


def split(a):
    hi = a.astype(BF16)
    return hi, (a - hi.astype(F32)).astype(BF16)


def mm_f32(a, b, dims):
    return lax.dot_general(a, b, dims, precision=lax.Precision.HIGHEST, preferred_element_type=F32)


def wide(parts):
    return jnp.concatenate(parts, axis=1)


def kernel(
    n_in, n_co, left_u, left_v, right_u, right_v, sketch, index, mask, basis, coeff,
    ug, vg, ru, rv, sk, skt, inv, lv, pb, pk, mix, wt, ct,
    ybuf, sbuf, r1, s2f, s2b, r2, yrow, yb,
    cbuf, csbuf, cr1, cs2f, cs2b, cr2, xm, scale,
    load_sem, vs_sem, vr_sem, us_sem, ur_sem, rs_send, rs_recv, ag_send, ag_recv,
):
    nx = n_co // 2
    ny = nx
    nz = n_in // ny
    tpd, nb, rk = left_v.shape
    nch, part_rows = ug.shape[0], ug.shape[3]
    tiles = tpd * n_co
    n_out, slots = right_u.shape[:2]
    rows = nb // n_in
    me_in = lax.axis_index("inner")
    me_co = lax.axis_index("cols")
    x, core = lax.div(me_co, 2), lax.rem(me_co, 2)
    z, y = lax.div(me_in, ny), lax.rem(me_in, ny)
    def co_at(dx):
        return lax.rem(x + dx, nx) * 2 + core

    partner = x * 2 + (1 - core)

    def z_at(dz):
        return lax.rem(z + dz, nz) * ny + y

    def y_at(dy):
        return z * ny + lax.rem(y + dy, ny)

    sends = []

    def remote(src, dst, s_sem, r_sem, **dev):
        return pltpu.make_async_remote_copy(
            src_ref=src, dst_ref=dst, send_sem=s_sem, recv_sem=r_sem,
            device_id=dev, device_id_type=MESH,
        )

    def go(copy):
        copy.start()
        sends.append(copy)

    own = pl.ds(me_co * tpd, tpd)
    early, late = [], []
    for j in range(n_out):
        early.append(pltpu.make_async_copy(sketch.at[j], sk.at[j], load_sem.at[j, 0]))
        early.append(pltpu.make_async_copy(right_v.at[j], rv.at[j], load_sem.at[j, 1]))
    late.append(pltpu.make_async_copy(left_v, vg.at[own], load_sem.at[n_out, 0]))
    for j in range(n_out):
        late.append(pltpu.make_async_copy(right_u.at[j], ru.at[j], load_sem.at[j, 2]))
    own_u = [
        pltpu.make_async_copy(left_u.at[:, :, c], ug.at[c, own], load_sem.at[n_out + 1, c]) for c in range(nch)
    ]
    for copy in early + late + own_u:
        copy.start()

    barrier = pltpu.get_barrier_semaphore()
    for dx in range(1, nx):
        pl.semaphore_signal(barrier, inc=1, device_id={"cols": co_at(dx)}, device_id_type=MESH)
    pl.semaphore_signal(barrier, inc=1, device_id={"cols": partner}, device_id_type=MESH)
    for dy in range(1, ny):
        pl.semaphore_signal(barrier, inc=1, device_id={"inner": y_at(dy)}, device_id_type=MESH)
    for dz in range(1, nz):
        pl.semaphore_signal(barrier, inc=1, device_id={"inner": z_at(dz)}, device_id_type=MESH)
    pl.semaphore_wait(barrier, nx - 1 + 1 + ny - 1 + nz - 1)

    for i in range(tpd):
        to = vg.at[me_co * tpd + i]
        for dx in range(1, nx):
            go(remote(left_v.at[i], to, vs_sem.at[i, dx], vr_sem.at[i, dx], cols=co_at(dx)))
        go(remote(left_v.at[i], to, vs_sem.at[i, 0], vr_sem.at[i, 0], cols=partner))
    for c in range(nch):
        for dx in range(1, nx):
            go(remote(left_u.at[:, :, c], ug.at[c, own], us_sem.at[c, dx], ur_sem.at[c, dx], cols=co_at(dx)))
        go(remote(left_u.at[:, :, c], ug.at[c, own], us_sem.at[c, 0], ur_sem.at[c, 0], cols=partner))

    def arrived(part, s_sem, r_sem):
        remote(part, part, s_sem, r_sem, cols=partner).wait_recv()

    for j in range(n_out):
        named = [lax.rem(index[j, s], tiles) for s in range(slots)]
        alive = [mask[j, s] for s in range(slots)]
        for k in range(tiles):
            at, live = jnp.int32(0), jnp.int32(0)
            for s in range(slots):
                hit = named[s] == k
                at = jnp.where(hit, s, at)
                live = jnp.where(hit, alive[s], live)
            inv[j, k] = at
            lv[j, k] = live

    for copy in early:
        copy.wait()

    @pl.loop(0, n_out)
    def _(j):
        skt[...] = jnp.transpose(sk[j])
        for s in range(0, slots, 2):
            out = mm(skt[...], wide([rv[j, s], rv[j, s + 1]]), NN)
            for i in range(2):
                hi, lo = split(out[:, i * rk : (i + 1) * rk])
                pb[j, s + i, :rk] = hi
                pb[j, s + i, rk:] = lo

    for copy in late:
        copy.wait()

    def pair(k):
        vt = jnp.transpose(vg[k])
        for first in range(0, n_out, 2):
            js = (first, first + 1)
            at = [inv[j, k] for j in js]
            out = mm(vt, wide([ru[j, s] for j, s in zip(js, at)]), NN)
            for i, (j, s) in enumerate(zip(js, at)):
                hi, lo = split(out[:, i * rk : (i + 1) * rk] * lv[j, k].astype(F32))
                both = wide([hi, lo])
                pk[j, k] = both
                probe = pb[j, s]
                mixed = mm(both, wide([probe, probe]), NT)
                mix[k, :, j * rk : (j + 1) * rk] = (mixed[:, :rk] + mixed[:, rk:]).astype(BF16)

    def fold(base):
        @pl.loop(0, tpd)
        def _(i):
            k = base + i
            for j in range(n_out):
                right = rv[j, inv[j, k]]
                hi, lo = split(mm(wide([right, right]), pk[j, k], NT))
                wt[j, k, 0] = hi
                wt[j, k, 1] = lo

    for i in range(tpd):
        pair(me_co * tpd + i)
    for i in range(tpd):
        k = partner * tpd + i
        arrived(vg.at[k], vs_sem.at[i, 0], vr_sem.at[i, 0])
        pair(k)

    def pass_on_v(i):
        for dx in range(1, nx):
            k = co_at(nx - dx) * tpd + i
            arrived(vg.at[k], vs_sem.at[i, dx], vr_sem.at[i, dx])
            go(remote(vg.at[k], vg.at[k], vs_sem.at[i, nx + dx], vr_sem.at[i, nx + dx], cols=partner))

    fold(me_co * tpd)
    for i in range(tpd):
        pass_on_v(i)
        for dx in range(1, nx):
            pair(co_at(nx - dx) * tpd + i)
        if i == tpd - 1:
            fold(partner * tpd)
        for dx in range(1, nx):
            k = (lax.rem(x + nx - dx, nx) * 2 + (1 - core)) * tpd + i
            arrived(vg.at[k], vs_sem.at[i, nx + dx], vr_sem.at[i, nx + dx])
            pair(k)
    for dx in range(1, nx):
        fold(co_at(nx - dx) * tpd)
    for copy in own_u:
        copy.wait()

    def block_u(c, position):
        return ug.at[c, pl.ds(position * tpd, tpd)]

    def pass_on_u(c):
        for dx in range(1, nx):
            part = block_u(c, co_at(nx - dx))
            arrived(part, us_sem.at[c, dx], ur_sem.at[c, dx])
            go(remote(part, part, us_sem.at[c, nx + dx], ur_sem.at[c, nx + dx], cols=partner))

    def gathered_u(c):
        arrived(block_u(c, partner), us_sem.at[c, 0], ur_sem.at[c, 0])
        for dx in range(1, nx):
            part = block_u(c, lax.rem(x + nx - dx, nx) * 2 + (1 - core))
            arrived(part, us_sem.at[c, nx + dx], ur_sem.at[c, nx + dx])

    def chunk_u(c):
        return wide([ug[c, k].reshape(nb // nch, rk) for k in range(tiles)])

    def scatter_first(phase, j, total, buf, sb, first):
        shape = (nz, ny, total.shape[0] // n_in, rk)
        buf[j] = total.reshape(shape)
        low = total.astype(BF16).reshape(shape)
        for yy in range(ny):
            sb[j, yy] = low[:, yy]
        for dy in range(1, ny):
            go(remote(
                sb.at[j, lax.rem(y + dy, ny)], first.at[j, dy],
                rs_send.at[phase, j, dy], rs_recv.at[phase, j, dy], inner=y_at(dy),
            ))

    def scatter_second(phase, j, buf, sb, first, sumf, sumb, second):
        total = buf[j, :, y]
        for dy in range(1, ny):
            part = first.at[j, dy]
            remote(part, part, rs_send.at[phase, j, dy], rs_recv.at[phase, j, dy], inner=y_at(dy)).wait_recv()
            total = total + first[j, dy].astype(F32)
        sumf[j] = total
        sumb[j] = total.astype(BF16)
        for dz in range(1, nz):
            go(remote(
                sumb.at[j, lax.rem(z + dz, nz)], second.at[j, dz],
                rs_send.at[phase, j, ny + dz], rs_recv.at[phase, j, ny + dz], inner=z_at(dz),
            ))

    def scatter_last(phase, j, sumf, second):
        total = sumf[j, z]
        for dz in range(1, nz):
            part = second.at[j, dz]
            remote(part, part, rs_send.at[phase, j, ny + dz], rs_recv.at[phase, j, ny + dz], inner=z_at(dz)).wait_recv()
            total = total + second[j, dz].astype(F32)
        return total

    def sketched(c):
        mixed = mix[...]
        mixed = mixed.reshape(tiles * rk, n_out * rk)
        total = mm(chunk_u(c), mixed, NN)
        for j in range(n_out):
            scatter_first(c, j, total[:, j * rk : (j + 1) * rk], ybuf.at[c], sbuf.at[c], r1.at[c])

    def second(c, j):
        scatter_second(c, j, ybuf.at[c], sbuf.at[c], r1.at[c], s2f.at[c], s2b.at[c], r2.at[c])

    def last(c, j):
        total = scatter_last(c, j, s2f.at[c], r2.at[c])
        yrow[j, c * part_rows : (c + 1) * part_rows] = total
        yb[c, j, me_in] = total.astype(BF16)
        part = yb.at[c, j, me_in]
        for dz in range(1, nz):
            go(remote(part, part, ag_send.at[c, j, 0, dz], ag_recv.at[c, j, 0, dz], inner=z_at(dz)))
        for dy in range(1, ny):
            go(remote(part, part, ag_send.at[c, j, dy, 0], ag_recv.at[c, j, dy, 0], inner=y_at(dy)))

    def spread(c, j):
        for dz in range(1, nz):
            part = yb.at[c, j, z_at(nz - dz)]
            remote(part, part, ag_send.at[c, j, 0, dz], ag_recv.at[c, j, 0, dz], inner=z_at(dz)).wait_recv()
            for dy in range(1, ny):
                go(remote(part, part, ag_send.at[c, j, dy, dz], ag_recv.at[c, j, dy, dz], inner=y_at(dy)))

    def complete(c, j):
        for dy in range(1, ny):
            for dz in range(nz):
                pos = lax.rem(z + nz - dz, nz) * ny + lax.rem(y + ny - dy, ny)
                part = yb.at[c, j, pos]
                remote(part, part, ag_send.at[c, j, dy, dz], ag_recv.at[c, j, dy, dz], inner=y_at(dy)).wait_recv()

    def tile_t(j, c):
        left = wide([wt[j, k, h] for h in range(2) for k in range(tiles)])
        right = chunk_u(c)
        hi, lo = split(mm(left, wide([right, right]), NT))
        ct[j, c, 0] = hi
        ct[j, c, 1] = lo

    def y_of(j):
        return jnp.concatenate([yb[c, j].reshape(nb // nch, rk) for c in range(nch)], axis=0)

    def back(j):
        left = wide([ct[j, c, h] for h in range(2) for c in range(nch)])
        right = y_of(j)
        total = mm(left, jnp.concatenate([right, right], axis=0), NN)
        scatter_first(nch, j, total, cbuf, csbuf, cr1)

    work = [(j, c) for c in range(nch) for j in range(n_out)]

    def some(n):
        for _ in range(n):
            if work:
                tile_t(*work.pop(0))

    for dx in range(1, nx):
        fold((lax.rem(x + nx - dx, nx) * 2 + (1 - core)) * tpd)
    for c in range(nch):
        pass_on_u(c)
        gathered_u(c)
        sketched(c)
        if c < nch - 1:
            some(2)
    for c in range(nch):
        for j in range(n_out):
            second(c, j)
        some(2)
    for c in range(nch):
        for j in range(n_out):
            last(c, j)
        if c < nch - 1:
            some(2)
    some(len(work))
    for c in range(nch):
        for j in range(n_out):
            spread(c, j)
    for j in range(n_out):
        for c in range(nch):
            complete(c, j)
        back(j)

    row_id = lax.broadcasted_iota(jnp.int32, (rk, rk), 0)
    col_id = lax.broadcasted_iota(jnp.int32, (rk, rk), 1)
    for j in range(n_out):
        summed = y_of(j)
        gram = mm(summed, summed, TN)
        diag = jnp.where(row_id == col_id, gram, 0.0)
        s_row = lax.rsqrt(jnp.sum(diag, axis=0, keepdims=True))
        s_col = lax.rsqrt(jnp.sum(diag, axis=1, keepdims=True))
        scale[j] = s_row
        xm[j] = gram * s_col * s_row

    sub8 = lax.broadcasted_iota(jnp.int32, (8, rk), 0)
    lane8 = lax.broadcasted_iota(jnp.int32, (8, rk), 1)

    def eliminate(start, stop):
        @pl.loop(start, stop)
        def _(b):
            base = pl.multiple_of(b * 8, 8)
            near = lane8 - base
            at = pl.ds(base, 8)
            slabs = [xm[j, at] for j in range(n_out)]
            cols = [
                [
                    jnp.broadcast_to(jnp.sum(jnp.where(near == i, slab, 0.0), axis=1, keepdims=True), (8, rk))
                    for i in range(8)
                ]
                for slab in slabs
            ]
            pivots = [jnp.ones((8, rk), F32)] * n_out
            for k in range(8):
                hot = jnp.where(near[:1] == k, 1.0, 0.0)
                for j in range(n_out):
                    column = cols[j][k]
                    pivots[j] = jnp.where(sub8 == k, column[k : k + 1], pivots[j])
                    weight = jnp.where(sub8 > k, column * (1.0 / column[k : k + 1]), 0.0)
                    slabs[j] = slabs[j] - weight * (slabs[j][k : k + 1] + hot)
                    for i in range(k + 1, 8):
                        cols[j][i] = cols[j][i] - weight * cols[j][i][k : k + 1]
            for j in range(n_out):
                ahead = jnp.where(near >= 8, slabs[j] / pivots[j], 0.0)
                unit = jnp.where(near == sub8, 1.0, jnp.where((near >= 0) & (near > sub8) & (near < 8), 0.0, slabs[j]))
                near_all = col_id - base
                clear = (row_id - base >= 8) & (near_all >= 0) & (near_all < 8)
                xm[j] = jnp.where(clear, 0.0, xm[j]) - mm_f32(ahead, unit, TN)
                xm[j, at] = slabs[j]

    blocks = rk // 8
    done = 0
    for j in range(n_out):
        upto = min(blocks, blocks * (5 + 2 * j) // 16)
        eliminate(done, upto)
        done = upto
        scatter_second(nch, j, cbuf, csbuf, cr1, cs2f, cs2b, cr2)
    eliminate(done, blocks)

    for j in range(n_out):
        left = xm[j]
        pivots = jnp.sum(jnp.where(row_id == col_id, left, 0.0), axis=1, keepdims=True)
        lower = jnp.where(col_id < row_id, left, jnp.where(row_id == col_id, 1.0, 0.0))
        inverse = lower * lax.rsqrt(pivots) * scale[j]
        basis[j] = mm_f32(yrow[j], inverse, NT) * math.sqrt(nb)
        coeff[j] = mm_f32(scatter_last(nch, j, cs2f, cr2), inverse, NT)

    for copy in sends:
        copy.wait_send()


def body(n_in, n_co, left_u, left_v, right_u, right_v, sketch, tile_index, slot_mask):
    n_out, slots, nb, rk = right_u.shape
    tpd = left_u.shape[0]
    tiles = tpd * n_co
    nx = n_co // 2
    ny = nx
    nz = n_in // ny
    rows = nb // n_in
    nch = 2 if rows % 32 == 0 else 1
    part_rows = rows // nch

    def wire(lead, height):
        return [
            pltpu.VMEM((*lead, n_out, nz, ny, height, rk), F32),
            pltpu.VMEM((*lead, n_out, ny, nz, height, rk), BF16),
            pltpu.VMEM((*lead, n_out, ny, nz, height, rk), BF16),
            pltpu.VMEM((*lead, n_out, nz, height, rk), F32),
            pltpu.VMEM((*lead, n_out, nz, height, rk), BF16),
            pltpu.VMEM((*lead, n_out, nz, height, rk), BF16),
        ]

    out = jax.ShapeDtypeStruct((n_out, rows, rk), F32)
    hbm = pl.BlockSpec(memory_space=pl.ANY)
    smem = pl.BlockSpec(memory_space=pltpu.SMEM)
    vmem = pl.BlockSpec(memory_space=pltpu.VMEM)
    return pl.pallas_call(
        functools.partial(kernel, n_in, n_co),
        out_shape=(out, out),
        in_specs=[hbm] * 5 + [smem] * 2,
        out_specs=(vmem, vmem),
        scratch_shapes=[
            pltpu.VMEM((nch, tiles, n_in, part_rows, rk), BF16),
            pltpu.VMEM((tiles, nb, rk), BF16),
            pltpu.VMEM((n_out, slots, nb, rk), BF16),
            pltpu.VMEM((n_out, slots, nb, rk), BF16),
            pltpu.VMEM((n_out, nb, rk), BF16),
            pltpu.VMEM((rk, nb), BF16),
            pltpu.SMEM((n_out, tiles), jnp.int32),
            pltpu.SMEM((n_out, tiles), jnp.int32),
            pltpu.VMEM((n_out, slots, 2 * rk, rk), BF16),
            pltpu.VMEM((n_out, tiles, rk, 2 * rk), BF16),
            pltpu.VMEM((tiles, rk, n_out * rk), BF16),
            pltpu.VMEM((n_out, tiles, 2, nb, rk), BF16),
            pltpu.VMEM((n_out, nch, 2, nb, nb // nch), BF16),
        ]
        + wire((nch,), part_rows)
        + [pltpu.VMEM((n_out, rows, rk), F32), pltpu.VMEM((nch, n_out, n_in, part_rows, rk), BF16)]
        + wire((), rows)
        + [
            pltpu.VMEM((n_out, rk, rk), F32),
            pltpu.VMEM((n_out, 1, rk), F32),
            pltpu.SemaphoreType.DMA((n_out + 2, 3)),
            pltpu.SemaphoreType.DMA((tpd, 2 * nx)),
            pltpu.SemaphoreType.DMA((tpd, 2 * nx)),
            pltpu.SemaphoreType.DMA((nch, 2 * nx)),
            pltpu.SemaphoreType.DMA((nch, 2 * nx)),
            pltpu.SemaphoreType.DMA((nch + 1, n_out, ny + nz)),
            pltpu.SemaphoreType.DMA((nch + 1, n_out, ny + nz)),
            pltpu.SemaphoreType.DMA((nch, n_out, ny, nz)),
            pltpu.SemaphoreType.DMA((nch, n_out, ny, nz)),
        ],
        compiler_params=pltpu.CompilerParams(
            collective_id=0, has_side_effects=True, vmem_limit_bytes=60 * 1024 * 1024
        ),
    )(left_u.reshape(tpd, n_in, nch, part_rows, rk), left_v, right_u, right_v, sketch, tile_index, slot_mask)


def solution(mesh):
    return jax.shard_map(
        functools.partial(body, mesh.shape["inner"], mesh.shape["cols"]),
        mesh=mesh,
        in_specs=(
            P(("inner", "cols"), None, None),
            P(("inner", "cols"), None, None),
            P("cols", "inner", None, None),
            P("cols", "inner", None, None),
            P("cols", None, None),
            P("cols", "inner"),
            P("cols", "inner"),
        ),
        out_specs=(P("cols", "inner", None), P("cols", "inner", None)),
        check_vma=False,
    )
```

```python
import functools
import math

import jax
import jax.numpy as jnp
from jax import lax
from jax.experimental import pallas as pl
from jax.experimental.pallas import tpu as pltpu
from jax.sharding import PartitionSpec as P

MESH = pl.DeviceIdType.MESH
F32 = jnp.float32
BF16 = jnp.bfloat16
NN = (((1,), (0,)), ((), ()))
NT = (((1,), (1,)), ((), ()))
TN = (((0,), (0,)), ((), ()))


def mm(a, b, dims):
    return lax.dot_general(a, b, dims, preferred_element_type=F32)


def split(a):
    hi = a.astype(BF16)
    return hi, (a - hi.astype(F32)).astype(BF16)


def mm_f32(a, b, dims):
    return lax.dot_general(a, b, dims, precision=lax.Precision.HIGHEST, preferred_element_type=F32)


def wide(parts):
    return jnp.concatenate(parts, axis=1)


def kernel(
    n_in, n_co, left_u, left_v, right_u, right_v, sketch, index_hbm, mask_hbm, outs,
    ug, vg, ru, rv, sk, skt, index, mask, inv, lv, pb, pk, mix, wt, ct,
    ybuf, sbuf, r1, s2f, s2b, r2, yrow, yb,
    cbuf, csbuf, cr1, cs2f, cs2b, cr2, xm, scale,
    load_sem, rv_sem, send_sem, v_sem, u_sem, sum_sem, ag_sem, back_sem,
):
    nx = n_co // 2
    ny = nx
    nz = n_in // ny
    tpd, nb, rk = left_v.shape
    nch, part_rows = ug.shape[0], ug.shape[3]
    groups = ct.shape[1]
    tiles = tpd * n_co
    n_out, slots = right_u.shape[:2]
    rows = nb // n_in
    me_in = lax.axis_index("inner")
    me_co = lax.axis_index("cols")
    x, core = lax.div(me_co, 2), lax.rem(me_co, 2)
    z, y = lax.div(me_in, ny), lax.rem(me_in, ny)
    def co_at(dx):
        return lax.rem(x + dx, nx) * 2 + core

    def other_at(dx):
        return lax.rem(x + dx, nx) * 2 + (1 - core)

    partner = other_at(0)

    def z_at(dz):
        return lax.rem(z + dz, nz) * ny + y

    def y_at(dy):
        return z * ny + lax.rem(y + dy, ny)

    V_OUT, U_OUT, SUM_Y, SUM_Z, GATHER, BACK_Y, BACK_Z = range(7)

    def remote(src, dst, kind, r_sem, **dev):
        return pltpu.make_async_remote_copy(
            src_ref=src, dst_ref=dst, send_sem=send_sem.at[kind], recv_sem=r_sem,
            device_id=dev, device_id_type=MESH,
        )

    def arrived(part, r_sem):
        pltpu.make_async_copy(part, part, r_sem).wait()

    own = pl.ds(me_co * tpd, tpd)
    tables = [pltpu.make_async_copy(index_hbm, index, load_sem.at[0]), pltpu.make_async_copy(mask_hbm, mask, load_sem.at[1])]
    first_sketch = pltpu.make_async_copy(sketch, sk, load_sem.at[2])
    rv_load = [pltpu.make_async_copy(right_v.at[j], rv.at[j], rv_sem.at[j]) for j in range(n_out)]
    own_v = pltpu.make_async_copy(left_v, vg.at[own], load_sem.at[3])
    ru_load = pltpu.make_async_copy(right_u, ru, load_sem.at[4])
    for copy in tables + [first_sketch] + rv_load + [own_v, ru_load]:
        copy.start()
    for c in range(nch):
        pltpu.make_async_copy(left_u.at[:, :, c], ug.at[c, own], load_sem.at[5]).start()

    barrier = pltpu.get_barrier_semaphore()
    for dx in range(1, nx):
        pl.semaphore_signal(barrier, inc=1, device_id={"cols": co_at(dx)}, device_id_type=MESH)
    pl.semaphore_signal(barrier, inc=1, device_id={"cols": partner}, device_id_type=MESH)
    for dy in range(1, ny):
        pl.semaphore_signal(barrier, inc=1, device_id={"inner": y_at(dy)}, device_id_type=MESH)
    for dz in range(1, nz):
        pl.semaphore_signal(barrier, inc=1, device_id={"inner": z_at(dz)}, device_id_type=MESH)
    pl.semaphore_wait(barrier, nx - 1 + 1 + ny - 1 + nz - 1)

    for i in range(tpd):
        for dx in range(1, nx):
            remote(left_v.at[i], vg.at[me_co * tpd + i], V_OUT, v_sem.at[0, i, dx], cols=co_at(dx)).start()
    remote(left_v, vg.at[own], V_OUT, v_sem.at[0, 0, 0], cols=partner).start()
    for c in range(nch):
        for dx in range(1, nx):
            remote(left_u.at[:, :, c], ug.at[c, own], U_OUT, u_sem.at[0, c, dx], cols=co_at(dx)).start()
    for c in range(nch):
        remote(left_u.at[:, :, c], ug.at[c, own], U_OUT, u_sem.at[0, 0, 0], cols=partner).start()

    for copy in tables:
        copy.wait()
    for j in range(n_out):
        named = [lax.rem(index[j, s], tiles) for s in range(slots)]
        alive = [mask[j, s] for s in range(slots)]
        for k in range(tiles):
            at, live = jnp.int32(0), jnp.int32(0)
            for s in range(slots):
                hit = named[s] == k
                at = jnp.where(hit, s, at)
                live = jnp.where(hit, alive[s], live)
            inv[j, k] = at
            lv[j, k] = live

    first_sketch.wait()

    @pl.loop(0, n_out)
    def _(j):
        skt[...] = jnp.transpose(sk[j])
        pltpu.make_async_copy(right_v.at[j], rv.at[j], rv_sem.at[j]).wait()
        for s in range(0, slots, 2):
            out = mm(skt[...], wide([rv[j, s], rv[j, s + 1]]), NN)
            for i in range(2):
                hi, lo = split(out[:, i * rk : (i + 1) * rk])
                pb[j, s + i, :rk] = hi
                pb[j, s + i, rk:] = lo

    own_v.wait()
    ru_load.wait()

    def pair(k):
        vt = jnp.transpose(vg[k])
        for first in range(0, n_out, 2):
            js = (first, first + 1)
            at = [inv[j, k] for j in js]
            out = mm(vt, wide([ru[j, s] for j, s in zip(js, at)]), NN)
            for i, (j, s) in enumerate(zip(js, at)):
                hi, lo = split(out[:, i * rk : (i + 1) * rk] * lv[j, k].astype(F32))
                both = wide([hi, lo])
                pk[j, k] = both
                probe = pb[j, s]
                mixed = mm(both, wide([probe, probe]), NT)
                mix[k, :, j * rk : (j + 1) * rk] = (mixed[:, :rk] + mixed[:, rk:]).astype(BF16)

    def fold_one(k):
        for j in range(n_out):
            right = rv[j, inv[j, k]]
            hi, lo = split(mm(wide([right, right]), pk[j, k], NT))
            wt[j, k, 0] = hi
            wt[j, k, 1] = lo

    folds = []

    def fold(n):
        todo = [folds.pop(0) for _ in range(min(n, len(folds)))]
        for k in todo:
            fold_one(k)

    for i in range(tpd):
        k = me_co * tpd + i
        pair(k)
        folds.append(k)
    arrived(vg.at[pl.ds(partner * tpd, tpd)], v_sem.at[0, 0, 0])
    for i in range(tpd):
        k = partner * tpd + i
        pair(k)
        folds.append(k)

    for i in range(tpd):
        for dx in range(1, nx):
            k = co_at(nx - dx) * tpd + i
            arrived(vg.at[k], v_sem.at[0, i, dx])
            remote(vg.at[k], vg.at[k], V_OUT, v_sem.at[1, i, dx], cols=partner).start()
        for dx in range(1, nx):
            k = co_at(nx - dx) * tpd + i
            pair(k)
            folds.append(k)
        for dx in range(1, nx):
            k = other_at(nx - dx) * tpd + i
            arrived(vg.at[k], v_sem.at[1, i, dx])
        for dx in range(1, nx):
            k = other_at(nx - dx) * tpd + i
            pair(k)
            folds.append(k)
        fold(max(1, 2 // tpd))
    pltpu.make_async_copy(left_v, vg.at[own], load_sem.at[5]).wait()
    arrived(vg.at[own], u_sem.at[0, 0, 0])

    def block_u(c, position):
        return ug.at[c, pl.ds(position * tpd, tpd)]

    def chunk_u(c):
        return wide([ug[c, k].reshape(nb // nch, rk) for k in range(tiles)])

    def sketched(c):
        total = mm(chunk_u(c), mix[...].reshape(tiles * rk, n_out * rk), NN)
        low = total.astype(BF16)
        for j in range(n_out):
            at = slice(j * rk, (j + 1) * rk)
            ybuf[c, :, :, j] = total[:, at].reshape(nz, ny, part_rows, rk)
            part = low[:, at].reshape(nz, ny, part_rows, rk)
            for yy in range(ny):
                sbuf[c, yy, :, j] = part[:, yy]
        for dy in range(1, ny):
            remote(sbuf.at[c, lax.rem(y + dy, ny)], r1.at[c, dy], SUM_Y, sum_sem.at[0, c], inner=y_at(dy)).start()

    def second(c):
        total = ybuf[c, :, y]
        arrived(r1.at[c, pl.ds(1, ny - 1)], sum_sem.at[0, c])
        for dy in range(1, ny):
            total = total + r1[c, dy].astype(F32)
        s2f[c] = total
        s2b[c] = total.astype(BF16)
        for dz in range(1, nz):
            remote(s2b.at[c, lax.rem(z + dz, nz)], r2.at[c, dz], SUM_Z, sum_sem.at[1, c], inner=z_at(dz)).start()

    def last(c):
        total = s2f[c, z]
        arrived(r2.at[c, pl.ds(1, nz - 1)], sum_sem.at[1, c])
        for dz in range(1, nz):
            total = total + r2[c, dz].astype(F32)
        yrow[:, c * part_rows : (c + 1) * part_rows] = total
        yb[c, me_in] = total.astype(BF16)
        part = yb.at[c, me_in]
        for dz in range(1, nz):
            remote(part, part, GATHER, ag_sem.at[c, dz], inner=z_at(dz)).start()
        for dy in range(1, ny):
            remote(part, part, GATHER, ag_sem.at[c, 0], inner=y_at(dy)).start()

    def spread(c):
        for dz in range(1, nz):
            part = yb.at[c, z_at(nz - dz)]
            arrived(part, ag_sem.at[c, dz])
            for dy in range(1, ny):
                remote(part, part, GATHER, ag_sem.at[c, 0], inner=y_at(dy)).start()

    def complete(c):
        arrived(yb.at[c, pl.ds(0, (ny - 1) * nz)], ag_sem.at[c, 0])

    span = nch // groups

    def tile_t(j, g):
        left = wide([wt[j, k, h] for h in range(2) for k in range(tiles)])
        right = jnp.concatenate([chunk_u(g * span + i) for i in range(span)], axis=0)
        for h, part in enumerate(split(mm(left, wide([right, right]), NT))):
            part = part.reshape(nz, ny, rows, nb // groups)
            for yy in range(ny):
                ct[j, g, h, yy] = part[:, yy].reshape(nz * rows, nb // groups)

    def y_of(j):
        return jnp.concatenate([yb[c, :, j].reshape(nb // nch, rk) for c in range(nch)], axis=0)

    def back(j):
        right = y_of(j)
        right = jnp.concatenate([right, right], axis=0)

        def share(yy):
            left = wide([ct[j, g, h, yy] for h in range(2) for g in range(groups)])
            return mm(left, right, NN).reshape(nz, rows, rk)

        for dy in range(1, ny):
            csbuf[j, dy] = share(lax.rem(y + dy, ny)).astype(BF16)
            remote(csbuf.at[j, dy], cr1.at[j, dy], BACK_Y, back_sem.at[0, j], inner=y_at(dy)).start()
        cbuf[j] = share(y)

    def back_second(j):
        total = cbuf[j]
        arrived(cr1.at[j, pl.ds(1, ny - 1)], back_sem.at[0, j])
        for dy in range(1, ny):
            total = total + cr1[j, dy].astype(F32)
        cs2f[j] = total
        cs2b[j] = total.astype(BF16)
        for dz in range(1, nz):
            remote(cs2b.at[j, lax.rem(z + dz, nz)], cr2.at[j, dz], BACK_Z, back_sem.at[1, j], inner=z_at(dz)).start()

    def back_last(j):
        total = cs2f[j, z]
        arrived(cr2.at[j, pl.ds(1, nz - 1)], back_sem.at[1, j])
        for dz in range(1, nz):
            total = total + cr2[j, dz].astype(F32)
        return total

    work = [(j, g) for g in range(groups) for j in range(n_out)]

    def some(n):
        for _ in range(n):
            if work:
                tile_t(*work.pop(0))

    for c in range(nch):
        for dx in range(1, nx):
            part = block_u(c, co_at(nx - dx))
            arrived(part, u_sem.at[0, c, dx])
            remote(part, part, U_OUT, u_sem.at[1, c, dx], cols=partner).start()
        fold(1)
        for dx in range(1, nx):
            arrived(block_u(c, other_at(nx - dx)), u_sem.at[1, c, dx])
        sketched(c)
    fold(len(folds))
    for c in range(nch):
        second(c)
        some(1)
    for c in range(nch):
        last(c)
        some(1)
    some(len(work))
    for c in range(nch):
        spread(c)
    for c in range(nch):
        complete(c)
    for j in range(n_out):
        back(j)

    row_id = lax.broadcasted_iota(jnp.int32, (rk, rk), 0)
    col_id = lax.broadcasted_iota(jnp.int32, (rk, rk), 1)
    for j in range(n_out):
        summed = y_of(j)
        gram = mm(summed, summed, TN)
        diag = jnp.where(row_id == col_id, gram, 0.0)
        s_row = lax.rsqrt(jnp.sum(diag, axis=0, keepdims=True))
        s_col = lax.rsqrt(jnp.sum(diag, axis=1, keepdims=True))
        scale[j] = s_row
        xm[j] = gram * s_col * s_row

    sub8 = lax.broadcasted_iota(jnp.int32, (8, rk), 0)
    lane8 = lax.broadcasted_iota(jnp.int32, (8, rk), 1)

    def eliminate(start, stop):
        @pl.loop(start, stop)
        def _(b):
            base = pl.multiple_of(b * 8, 8)
            near = lane8 - base
            at = pl.ds(base, 8)
            slabs = [xm[j, at] for j in range(n_out)]
            cols = [
                [
                    jnp.broadcast_to(jnp.sum(jnp.where(near == i, slab, 0.0), axis=1, keepdims=True), (8, rk))
                    for i in range(8)
                ]
                for slab in slabs
            ]
            pivots = [jnp.ones((8, rk), F32)] * n_out
            for k in range(8):
                hot = jnp.where(near[:1] == k, 1.0, 0.0)
                for j in range(n_out):
                    column = cols[j][k]
                    pivots[j] = jnp.where(sub8 == k, column[k : k + 1], pivots[j])
                    weight = jnp.where(sub8 > k, column * (1.0 / column[k : k + 1]), 0.0)
                    slabs[j] = slabs[j] - weight * (slabs[j][k : k + 1] + hot)
                    for i in range(k + 1, 8):
                        cols[j][i] = cols[j][i] - weight * cols[j][i][k : k + 1]
            for j in range(n_out):
                ahead = jnp.where(near >= 8, slabs[j] / pivots[j], 0.0)
                unit = jnp.where(near == sub8, 1.0, jnp.where((near >= 0) & (near > sub8) & (near < 8), 0.0, slabs[j]))
                near_all = col_id - base
                clear = (row_id - base >= 8) & (near_all >= 0) & (near_all < 8)
                xm[j] = jnp.where(clear, 0.0, xm[j]) - mm_f32(ahead, unit, TN)
                xm[j, at] = slabs[j]

    blocks = rk // 8
    done = 0
    for j in range(n_out):
        upto = min(blocks, blocks * (5 + 2 * j) // 16)
        eliminate(done, upto)
        done = upto
        back_second(j)
    eliminate(done, blocks)

    for j in range(n_out):
        left = xm[j]
        pivots = jnp.sum(jnp.where(row_id == col_id, left, 0.0), axis=1, keepdims=True)
        lower = jnp.where(col_id < row_id, left, jnp.where(row_id == col_id, 1.0, 0.0))
        inverse = lower * lax.rsqrt(pivots) * scale[j]
        outs[0, j] = mm_f32(yrow[j], inverse, NT)
        outs[1, j] = mm_f32(back_last(j) * 0.5, inverse, NT)

    def gone(ref, kind):
        pltpu.make_async_copy(ref, ref, send_sem.at[kind]).wait()

    gone(vg.at[pl.ds(0, tiles - tpd)], V_OUT)
    gone(vg.at[pl.ds(0, tiles - tpd)], U_OUT)
    gone(r1.at[:, pl.ds(1, ny - 1)], SUM_Y)
    gone(r2.at[:, pl.ds(1, nz - 1)], SUM_Z)
    gone(yb.at[:, pl.ds(0, n_in - 1)], GATHER)
    gone(cr1.at[:, pl.ds(1, ny - 1)], BACK_Y)
    gone(cr2.at[:, pl.ds(1, nz - 1)], BACK_Z)


def body(n_in, n_co, left_u, left_v, right_u, right_v, sketch, tile_index, slot_mask):
    n_out, slots, nb, rk = right_u.shape
    tpd = left_u.shape[0]
    tiles = tpd * n_co
    nx = n_co // 2
    ny = nx
    nz = n_in // ny
    rows = nb // n_in
    nch = rows // 16
    part_rows = rows // nch
    groups = max(1, nch // 2)
    both = pl.pallas_call(
        functools.partial(kernel, n_in, n_co),
        out_shape=jax.ShapeDtypeStruct((2, n_out, rows, rk), F32),
        in_specs=[pl.BlockSpec(memory_space=pl.ANY)] * 7,
        out_specs=pl.BlockSpec(memory_space=pltpu.VMEM),
        scratch_shapes=[
            pltpu.VMEM((nch, tiles, n_in, part_rows, rk), BF16),
            pltpu.VMEM((tiles, nb, rk), BF16),
            pltpu.VMEM((n_out, slots, nb, rk), BF16),
            pltpu.VMEM((n_out, slots, nb, rk), BF16),
            pltpu.VMEM((n_out, nb, rk), BF16),
            pltpu.VMEM((rk, nb), BF16),
            pltpu.SMEM((n_out, slots), jnp.int32),
            pltpu.SMEM((n_out, slots), jnp.int32),
            pltpu.SMEM((n_out, tiles), jnp.int32),
            pltpu.SMEM((n_out, tiles), jnp.int32),
            pltpu.VMEM((n_out, slots, 2 * rk, rk), BF16),
            pltpu.VMEM((n_out, tiles, rk, 2 * rk), BF16),
            pltpu.VMEM((tiles, rk, n_out * rk), BF16),
            pltpu.VMEM((n_out, tiles, 2, nb, rk), BF16),
            pltpu.VMEM((n_out, groups, 2, ny, nz * rows, nb // groups), BF16),
            pltpu.VMEM((nch, nz, ny, n_out, part_rows, rk), F32),
            pltpu.VMEM((nch, ny, nz, n_out, part_rows, rk), BF16),
            pltpu.VMEM((nch, ny, nz, n_out, part_rows, rk), BF16),
            pltpu.VMEM((nch, nz, n_out, part_rows, rk), F32),
            pltpu.VMEM((nch, nz, n_out, part_rows, rk), BF16),
            pltpu.VMEM((nch, nz, n_out, part_rows, rk), BF16),
            pltpu.VMEM((n_out, rows, rk), F32),
            pltpu.VMEM((nch, n_in, n_out, part_rows, rk), BF16),
            pltpu.VMEM((n_out, nz, rows, rk), F32),
            pltpu.VMEM((n_out, ny, nz, rows, rk), BF16),
            pltpu.VMEM((n_out, ny, nz, rows, rk), BF16),
            pltpu.VMEM((n_out, nz, rows, rk), F32),
            pltpu.VMEM((n_out, nz, rows, rk), BF16),
            pltpu.VMEM((n_out, nz, rows, rk), BF16),
            pltpu.VMEM((n_out, rk, rk), F32),
            pltpu.VMEM((n_out, 1, rk), F32),
            pltpu.SemaphoreType.DMA((6,)),
            pltpu.SemaphoreType.DMA((n_out,)),
            pltpu.SemaphoreType.DMA((7,)),
            pltpu.SemaphoreType.DMA((2, tpd, nx)),
            pltpu.SemaphoreType.DMA((2, nch, nx)),
            pltpu.SemaphoreType.DMA((2, nch)),
            pltpu.SemaphoreType.DMA((nch, nz)),
            pltpu.SemaphoreType.DMA((2, n_out)),
        ],
        compiler_params=pltpu.CompilerParams(
            collective_id=0, has_side_effects=True, vmem_limit_bytes=60 * 1024 * 1024
        ),
    )(left_u.reshape(tpd, n_in, nch, part_rows, rk), left_v, right_u, right_v, sketch, tile_index, slot_mask)
    return both[0] * math.sqrt(nb), both[1] * 2.0


def solution(mesh):
    return jax.shard_map(
        functools.partial(body, mesh.shape["inner"], mesh.shape["cols"]),
        mesh=mesh,
        in_specs=(
            P(("inner", "cols"), None, None),
            P(("inner", "cols"), None, None),
            P("cols", "inner", None, None),
            P("cols", "inner", None, None),
            P("cols", None, None),
            P("cols", "inner"),
            P("cols", "inner"),
        ),
        out_specs=(P("cols", "inner", None), P("cols", "inner", None)),
        check_vma=False,
    )
```

```python
import functools
import math

import jax
import jax.numpy as jnp
from jax import lax
from jax.experimental import pallas as pl
from jax.experimental.pallas import tpu as pltpu
from jax.sharding import PartitionSpec as P

MESH = pl.DeviceIdType.MESH
F32 = jnp.float32
BF16 = jnp.bfloat16
NN = (((1,), (0,)), ((), ()))
NT = (((1,), (1,)), ((), ()))
TN = (((0,), (0,)), ((), ()))


def mm(a, b, dims):
    return lax.dot_general(a, b, dims, preferred_element_type=F32)


def split(a):
    hi = a.astype(BF16)
    return hi, (a - hi.astype(F32)).astype(BF16)


LEFT = (0, 0, 1, 1, 0, 2)
RIGHT = (0, 1, 0, 1, 2, 0)


def stack(a, order):
    first = a.astype(BF16).astype(F32)
    second = (a - first).astype(BF16).astype(F32)
    parts = (first, second, a - first - second)
    return jnp.concatenate([parts[i] for i in order], axis=0).astype(BF16)


def wide(parts):
    return jnp.concatenate(parts, axis=1)


def kernel(
    n_in, n_co, left_u, left_v, right_u, right_v, sketch, index_hbm, mask_hbm, outs,
    ug, vg, ru, rv, sk, skt, index, mask, inv, lv, pb, pk, mix, wt, ct,
    ybuf, sbuf, r1, s2f, s2b, r2, r3, yrow, yb,
    cbuf, csbuf, cr1, cs2f, cs2b, cr2, xm, scale, inverse,
    load_sem, rv_sem, send_sem, v_sem, u_sem, sum_sem, ag_sem, back_sem,
):
    nx = n_co // 2
    ny = nx
    nz = n_in // ny
    tpd, nb, rk = left_v.shape
    nch, part_rows = ug.shape[0], ug.shape[3]
    groups = ct.shape[1]
    cuts = cbuf.shape[1]
    tiles = tpd * n_co
    n_out, slots = right_u.shape[:2]
    rows = nb // n_in
    me_in = lax.axis_index("inner")
    me_co = lax.axis_index("cols")
    x, core = lax.div(me_co, 2), lax.rem(me_co, 2)
    z, y = lax.div(me_in, ny), lax.rem(me_in, ny)
    def co_at(dx):
        return lax.rem(x + dx, nx) * 2 + core

    def other_at(dx):
        return lax.rem(x + dx, nx) * 2 + (1 - core)

    partner = other_at(0)

    def z_at(dz):
        return lax.rem(z + dz, nz) * ny + y

    def y_at(dy):
        return z * ny + lax.rem(y + dy, ny)

    half = nz // 2
    depth = jnp.minimum(z, nz - 1 - z)
    inwards = jnp.where(z < half, 1, -1)
    inner_at = (z + inwards) * ny + y
    outer_at = (z - inwards) * ny + y

    parts = []
    for c in range(nch):
        n = n_out // 2 if c < nch - 1 else 1
        parts += [(c, j, n) for j in range(0, n_out, n)]
    V_OUT, U_OUT, SUM_Y, SUM_Z, GATHER_Z, GATHER_Y, BACK_Y, BACK_Z = range(8)

    def remote(src, dst, kind, r_sem, **dev):
        return pltpu.make_async_remote_copy(
            src_ref=src, dst_ref=dst, send_sem=send_sem.at[kind], recv_sem=r_sem,
            device_id=dev, device_id_type=MESH,
        )

    def arrived(part, r_sem):
        pltpu.make_async_copy(part, part, r_sem).wait()

    own = pl.ds(me_co * tpd, tpd)
    tables = [pltpu.make_async_copy(index_hbm, index, load_sem.at[0]), pltpu.make_async_copy(mask_hbm, mask, load_sem.at[1])]
    first_sketch = pltpu.make_async_copy(sketch, sk, load_sem.at[2])
    rv_load = [pltpu.make_async_copy(right_v.at[j], rv.at[j], rv_sem.at[j]) for j in range(n_out)]
    own_v = pltpu.make_async_copy(left_v, vg.at[own], load_sem.at[3])
    ru_load = pltpu.make_async_copy(right_u, ru, load_sem.at[4])
    for copy in tables + [first_sketch] + rv_load[:2]:
        copy.start()

    barrier = pltpu.get_barrier_semaphore()
    for dx in range(1, nx):
        pl.semaphore_signal(barrier, inc=1, device_id={"cols": co_at(dx)}, device_id_type=MESH)
    pl.semaphore_signal(barrier, inc=1, device_id={"cols": partner}, device_id_type=MESH)
    for dy in range(1, ny):
        pl.semaphore_signal(barrier, inc=1, device_id={"inner": y_at(dy)}, device_id_type=MESH)
    for dz in range(1, nz):
        pl.semaphore_signal(barrier, inc=1, device_id={"inner": z_at(dz)}, device_id_type=MESH)
    pl.semaphore_wait(barrier, nx - 1 + 1 + ny - 1 + nz - 1)

    for i in range(tpd):
        for dx in range(1, nx):
            remote(left_v.at[i], vg.at[me_co * tpd + i], V_OUT, v_sem.at[1 + 2 * ((dx - 1) * tpd + i)], cols=co_at(dx)).start()
    for c in range(nch):
        for dx in range(1, nx):
            remote(left_u.at[:, :, c], ug.at[c, own], U_OUT, u_sem.at[1 + 2 * ((dx - 1) * nch + c)], cols=co_at(dx)).start()
    for copy in rv_load[2:] + [own_v]:
        copy.start()
    remote(left_v, vg.at[own], V_OUT, v_sem.at[0], cols=partner).start()
    ru_load.start()
    for c in range(nch):
        pltpu.make_async_copy(left_u.at[:, :, c], ug.at[c, own], load_sem.at[5]).start()
    for c in range(nch):
        remote(left_u.at[:, :, c], ug.at[c, own], U_OUT, u_sem.at[0], cols=partner).start()

    for copy in tables:
        copy.wait()
    for j in range(n_out):
        named = [lax.rem(index[j, s], tiles) for s in range(slots)]
        alive = [mask[j, s] for s in range(slots)]
        for k in range(tiles):
            at, live = jnp.int32(0), jnp.int32(0)
            for s in range(slots):
                hit = named[s] == k
                at = jnp.where(hit, s, at)
                live = jnp.where(hit, alive[s], live)
            inv[j, k] = at
            lv[j, k] = live

    first_sketch.wait()

    @pl.loop(0, n_out)
    def _(j):
        skt[...] = jnp.transpose(sk[j])
        pltpu.make_async_copy(right_v.at[j], rv.at[j], rv_sem.at[j]).wait()
        for s in range(0, slots, 2):
            out = mm(skt[...], wide([rv[j, s], rv[j, s + 1]]), NN)
            for i in range(2):
                hi, lo = split(out[:, i * rk : (i + 1) * rk])
                pb[j, s + i, :rk] = hi
                pb[j, s + i, rk:] = lo

    own_v.wait()
    ru_load.wait()

    def pair(k):
        vt = jnp.transpose(vg[k])
        for first in range(0, n_out, 2):
            js = (first, first + 1)
            at = [inv[j, k] for j in js]
            out = mm(vt, wide([ru[j, s] for j, s in zip(js, at)]), NN)
            for i, (j, s) in enumerate(zip(js, at)):
                hi, lo = split(out[:, i * rk : (i + 1) * rk] * lv[j, k].astype(F32))
                both = wide([hi, lo])
                pk[j, k] = both
                probe = pb[j, s]
                mixed = mm(both, wide([probe, probe]), NT)
                mix[k, :, j * rk : (j + 1) * rk] = (mixed[:, :rk] + mixed[:, rk:]).astype(BF16)

    def fold_one(k):
        for j in range(n_out):
            right = rv[j, inv[j, k]]
            wt[j, k, 0], wt[j, k, 1] = split(mm(wide([right, right]), pk[j, k], NT))

    folds = []

    def fold(n):
        todo = [folds.pop(0) for _ in range(min(n, len(folds)))]
        for k in todo:
            fold_one(k)

    for i in range(tpd):
        k = me_co * tpd + i
        pair(k)
        folds.append(k)
    arrived(vg.at[pl.ds(partner * tpd, tpd)], v_sem.at[0])
    for i in range(tpd):
        k = partner * tpd + i
        pair(k)
        folds.append(k)

    for i in range(tpd):
        for dx in range(1, nx):
            k = co_at(nx - dx) * tpd + i
            arrived(vg.at[k], v_sem.at[1 + 2 * ((dx - 1) * tpd + i)])
            remote(vg.at[k], vg.at[k], V_OUT, v_sem.at[2 + 2 * ((dx - 1) * tpd + i)], cols=partner).start()
        for dx in range(1, nx):
            k = co_at(nx - dx) * tpd + i
            pair(k)
            folds.append(k)
        fold(1)
        for dx in range(1, nx):
            k = other_at(nx - dx) * tpd + i
            arrived(vg.at[k], v_sem.at[2 + 2 * ((dx - 1) * tpd + i)])
        for dx in range(1, nx):
            k = other_at(nx - dx) * tpd + i
            pair(k)
            folds.append(k)
        if i < tpd - 1:
            fold(1)
    pltpu.make_async_copy(left_v, vg.at[own], load_sem.at[5]).wait()
    arrived(vg.at[own], u_sem.at[0])

    def block_u(c, position):
        return ug.at[c, pl.ds(position * tpd, tpd)]

    def chunk_u(c):
        return wide([ug[c, k].reshape(nb // nch, rk) for k in range(tiles)])

    def sketched(c):
        total = mm(chunk_u(c), mix[...].reshape(tiles * rk, n_out * rk), NN)
        low = total.astype(BF16)
        for j in range(n_out):
            at = slice(j * rk, (j + 1) * rk)
            shape = (nz, ny, part_rows, rk)
            full = total[:, at].reshape(shape)
            part = low[:, at].reshape(shape)
            for yy in range(ny):
                ybuf[c, yy, :, j] = full[:, yy]
                sbuf[c, yy, :, j] = part[:, yy]
        for q, (of, first, n) in enumerate(parts):
            if of == c:
                at = pl.ds(first, n)
                for dy in range(1, ny):
                    remote(
                        sbuf.at[c, lax.rem(y + dy, ny), :, at], r1.at[c, dy, :, at],
                        SUM_Y, sum_sem.at[0, q], inner=y_at(dy),
                    ).start()

    def second(q):
        c, first, n = parts[q]
        at = pl.ds(first, n)
        arrived(r1.at[c, pl.ds(1, ny - 1), :, at], sum_sem.at[0, q])
        total = ybuf[c, y, :, at]
        for dy in range(1, ny):
            total = total + r1[c, dy, :, at].astype(F32)
        s2f[c, :, at] = total
        if half > 1:
            @pl.when(depth == 0)
            def _():
                s2b[c, :, at] = total.astype(BF16)
                remote(s2b.at[c, :, at], r2.at[c, :, at], SUM_Z, sum_sem.at[1, q], inner=inner_at).start()

    def third(q, level):
        c, first, n = parts[q]
        at = pl.ds(first, n)

        @pl.when(depth == level)
        def _():
            arrived(r2.at[c, :, at], sum_sem.at[1, q])
            total = s2f[c, :, at] + r2[c, :, at].astype(F32)
            s2b[c, :, at] = total.astype(BF16)
            land, sem = (r2, 1) if level < half - 1 else (r3, 2)
            remote(s2b.at[c, :, at], land.at[c, :, at], SUM_Z, sum_sem.at[sem, q], inner=inner_at).start()
            s2f[c, :, at] = total

    def to_y(q):
        c, first, n = parts[q]
        part = yb.at[c, y, :, pl.ds(first, n)]
        for dy in range(1, ny):
            remote(part, part, GATHER_Y, ag_sem.at[q], inner=y_at(dy)).start()

    def to_outer(q):
        c, first, n = parts[q]
        part = yb.at[c, y, :, pl.ds(first, n)]
        remote(part, part, GATHER_Z, sum_sem.at[1, q], inner=outer_at).start()

    def last(q):
        c, first, n = parts[q]
        at = pl.ds(first, n)

        @pl.when(depth == half - 1)
        def _():
            arrived(r3.at[c, :, at], sum_sem.at[2, q])
            total = s2f[c, :, at] + r3[c, :, at].astype(F32)
            yb[c, y, :, at] = total.astype(BF16)
            if half > 1:
                to_outer(q)
            to_y(q)
            s2f[c, :, at] = total
            yrow[at, c * part_rows : (c + 1) * part_rows] = s2f[c, z, at]

    def spread(q, level):
        c, first, n = parts[q]
        at = pl.ds(first, n)

        @pl.when(depth == level)
        def _():
            arrived(yb.at[c, y, :, at], sum_sem.at[1, q])
            if level > 0:
                to_outer(q)
            to_y(q)
            yrow[at, c * part_rows : (c + 1) * part_rows] = yb[c, y, z, at].astype(F32)

    def complete(q):
        c, first, n = parts[q]
        arrived(yb.at[c, pl.ds(0, ny - 1), :, pl.ds(first, n)], ag_sem.at[q])

    span = nch // groups

    def tile_t(j, g):
        left = wide([wt[j, k, h] for h in range(2) for k in range(tiles)])
        right = jnp.concatenate([chunk_u(g * span + i) for i in range(span)], axis=0)
        for h, part in enumerate(split(mm(left, wide([right, right]), NT))):
            part = part.reshape(nz, ny, rows, nb // groups)
            for yy in range(ny):
                ct[j, g, h, yy] = part[:, yy].reshape(nz * rows, nb // groups)

    def y_chunk(c, j):
        return jnp.concatenate([yb[c, yy, zz, j] for zz in range(nz) for yy in range(ny)], axis=0)

    def y_of(j):
        return jnp.concatenate([y_chunk(c, j) for c in range(nch)], axis=0)

    def back(j):
        right = y_of(j)
        right = jnp.concatenate([right, right], axis=0)

        def share(yy):
            left = wide([ct[j, g, h, yy] for h in range(2) for g in range(groups)])
            return mm(left, right, NN).reshape(nz, cuts, rows // cuts, rk)

        for dy in range(1, ny):
            part = share(lax.rem(y + dy, ny)).astype(BF16)
            for p in range(cuts):
                csbuf[j, p, dy] = part[:, p]
                remote(
                    csbuf.at[j, p, dy], cr1.at[j, p, dy], BACK_Y, back_sem.at[0, j, p], inner=y_at(dy)
                ).start()
        part = share(y)
        for p in range(cuts):
            cbuf[j, p] = part[:, p]

    def back_second(j, p):
        total = cbuf[j, p]
        arrived(cr1.at[j, p, pl.ds(1, ny - 1)], back_sem.at[0, j, p])
        for dy in range(1, ny):
            total = total + cr1[j, p, dy].astype(F32)
        cs2f[j, p] = total
        cs2b[j, p] = total.astype(BF16)
        for dz in range(1, nz):
            remote(
                cs2b.at[j, p, lax.rem(z + dz, nz)], cr2.at[j, p, dz], BACK_Z, back_sem.at[1, j, p], inner=z_at(dz)
            ).start()

    def back_last(j):
        parts = []
        for p in range(cuts):
            total = cs2f[j, p, z]
            arrived(cr2.at[j, p, pl.ds(1, nz - 1)], back_sem.at[1, j, p])
            for dz in range(1, nz):
                total = total + cr2[j, p, dz].astype(F32)
            parts.append(total)
        return jnp.concatenate(parts, axis=0)

    work = [(j, g) for g in range(groups) for j in range(n_out)]

    def pass_on_u(c):
        for dx in range(1, nx):
            part = block_u(c, co_at(nx - dx))
            arrived(part, u_sem.at[1 + 2 * ((dx - 1) * nch + c)])
            remote(part, part, U_OUT, u_sem.at[2 + 2 * ((dx - 1) * nch + c)], cols=partner).start()

    def gram(c):
        for j in range(n_out):
            part = y_chunk(c, j)
            total = mm(part, part, TN)
            xm[j] = total if c == 0 else xm[j] + total

    pass_on_u(0)
    for c in range(nch):
        if c == 0:
            fold(1)
        if c < nch - 1:
            pass_on_u(c + 1)
        if c == nch - 1:
            fold(2)
        for dx in range(1, nx):
            arrived(block_u(c, other_at(nx - dx)), u_sem.at[2 + 2 * ((dx - 1) * nch + c)])
        sketched(c)
        if c == 1:
            fold(1)

    count = len(parts)
    stages = [second]
    stages += [functools.partial(third, level=i) for i in range(1, half)]
    stages += [last]
    stages += [functools.partial(spread, level=i) for i in range(half - 2, -1, -1)]
    times = {}
    for q, (c, first, n) in enumerate(parts):
        start = 1.4 * (c + 0.7 * first / n_out)
        for i in range(len(stages)):
            times[i, q] = start + (0.0, *[3.1 + 3.6 * h for h in range(half)], *[2.4 * (h + 1) + 3.6 * half - 0.5 for h in range(half - 1)])[i]
    order = sorted(times, key=times.get)
    def products(here):
        @pl.when(here)
        def _():
            for j, g in work:
                tile_t(j, g)

    for i, q in order:
        stages[i](q)
        if (i, q) == (0, 1):
            fold(len(folds))
        if (i, q) == (0, count - 1):
            products(depth < half - 1)
        if (i, q) == (half, count - 1):
            products(depth == half - 1)
    for c in range(nch):
        for q in range(count):
            if parts[q][0] == c:
                complete(q)
                if c == nch - 1:
                    back(parts[q][1])
        if c < nch - 1:
            gram(c)
    gram(nch - 1)
    row_id = lax.broadcasted_iota(jnp.int32, (rk, rk), 0)
    col_id = lax.broadcasted_iota(jnp.int32, (rk, rk), 1)
    for j in range(n_out):
        whole = xm[j]
        diag = jnp.where(row_id == col_id, whole, 0.0)
        s_row = lax.rsqrt(jnp.sum(diag, axis=0, keepdims=True))
        s_col = lax.rsqrt(jnp.sum(diag, axis=1, keepdims=True))
        scale[j] = s_row
        xm[j] = whole * s_col * s_row

    sub8 = lax.broadcasted_iota(jnp.int32, (8, rk), 0)
    lane8 = lax.broadcasted_iota(jnp.int32, (8, rk), 1)

    def eliminate(start, stop):
        @pl.loop(start, stop)
        def _(b):
            eliminate_block(b)

    def eliminate_block(b):
        base = b * 8 if isinstance(b, int) else pl.multiple_of(b * 8, 8)
        near = lane8 - base
        at = pl.ds(base, 8)
        slabs = [xm[j, at] for j in range(n_out)]
        cols = [
            [
                jnp.broadcast_to(jnp.sum(jnp.where(near == i, slab, 0.0), axis=1, keepdims=True), (8, rk))
                for i in range(8)
            ]
            for slab in slabs
        ]
        pivots = [jnp.ones((8, rk), F32)] * n_out
        for k in range(8):
            hot = jnp.where(near[:1] == k, 1.0, 0.0)
            for j in range(n_out):
                column = cols[j][k]
                pivots[j] = jnp.where(sub8 == k, column[k : k + 1], pivots[j])
                weight = jnp.where(sub8 > k, column * (1.0 / column[k : k + 1]), 0.0)
                slabs[j] = slabs[j] - weight * (slabs[j][k : k + 1] + hot)
                for i in range(k + 1, 8):
                    cols[j][i] = cols[j][i] - weight * cols[j][i][k : k + 1]
        for j in range(n_out):
            ahead = jnp.where(near >= 8, slabs[j] / pivots[j], 0.0)
            unit = jnp.where(near == sub8, 1.0, jnp.where((near >= 0) & (near > sub8) & (near < 8), 0.0, slabs[j]))
            near_all = col_id - base
            clear = (row_id - base >= 8) & (near_all >= 0) & (near_all < 8)
            xm[j] = jnp.where(clear, 0.0, xm[j]) - mm(stack(ahead, LEFT), stack(unit, RIGHT), TN)
            xm[j, at] = slabs[j]

    blocks = rk // 8
    pieces = [(j, p) for j in range(n_out) for p in range(cuts)]
    done = 0
    for n, (j, p) in enumerate(pieces):
        upto = blocks * (2 * len(pieces) + 10 * n) // (16 * len(pieces))
        if upto > done:
            eliminate(done, upto)
            done = upto
        back_second(j, p)
    eliminate(done, blocks)

    for j in range(n_out):
        left = xm[j]
        pivots = jnp.sum(jnp.where(row_id == col_id, left, 0.0), axis=1, keepdims=True)
        lower = jnp.where(col_id < row_id, left, jnp.where(row_id == col_id, 1.0, 0.0))
        hi, lo = split(lower * lax.rsqrt(pivots) * scale[j])
        inverse[j] = wide([hi, lo, hi])
        hi, lo = split(yrow[j])
        outs[0, j] = mm(wide([hi, hi, lo]), inverse[j], NT)
    for j in range(n_out):
        hi, lo = split(back_last(j) * 0.5)
        outs[1, j] = mm(wide([hi, hi, lo]), inverse[j], NT)

    def gone(ref, kind):
        pltpu.make_async_copy(ref, ref, send_sem.at[kind]).wait()

    gone(vg.at[pl.ds(0, tiles - tpd)], V_OUT)
    gone(vg.at[pl.ds(0, tiles - tpd)], U_OUT)
    gone(r1.at[:, pl.ds(1, ny - 1)], SUM_Y)
    gone(s2b, SUM_Z)
    if half > 1:
        @pl.when(depth > 0)
        def _():
            gone(yb.at[:, 0], GATHER_Z)
    gone(yb.at[:, pl.ds(0, ny - 1)], GATHER_Y)
    gone(cr1.at[:, :, pl.ds(1, ny - 1)], BACK_Y)
    gone(cr2.at[:, :, pl.ds(1, nz - 1)], BACK_Z)


def body(n_in, n_co, left_u, left_v, right_u, right_v, sketch, tile_index, slot_mask):
    n_out, slots, nb, rk = right_u.shape
    tpd = left_u.shape[0]
    tiles = tpd * n_co
    nx = n_co // 2
    ny = nx
    nz = n_in // ny
    rows = nb // n_in
    nch = rows // 16
    part_rows = rows // nch
    groups = max(1, nch // 2)
    count = 2 * (nch - 1) + n_out
    cuts = 2 if rows % 32 == 0 else 1
    both = pl.pallas_call(
        functools.partial(kernel, n_in, n_co),
        out_shape=jax.ShapeDtypeStruct((2, n_out, rows, rk), F32),
        in_specs=[pl.BlockSpec(memory_space=pl.ANY)] * 7,
        out_specs=pl.BlockSpec(memory_space=pltpu.VMEM),
        scratch_shapes=[
            pltpu.VMEM((nch, tiles, n_in, part_rows, rk), BF16),
            pltpu.VMEM((tiles, nb, rk), BF16),
            pltpu.VMEM((n_out, slots, nb, rk), BF16),
            pltpu.VMEM((n_out, slots, nb, rk), BF16),
            pltpu.VMEM((n_out, nb, rk), BF16),
            pltpu.VMEM((rk, nb), BF16),
            pltpu.SMEM((n_out, slots), jnp.int32),
            pltpu.SMEM((n_out, slots), jnp.int32),
            pltpu.SMEM((n_out, tiles), jnp.int32),
            pltpu.SMEM((n_out, tiles), jnp.int32),
            pltpu.VMEM((n_out, slots, 2 * rk, rk), BF16),
            pltpu.VMEM((n_out, tiles, rk, 2 * rk), BF16),
            pltpu.VMEM((tiles, rk, n_out * rk), BF16),
            pltpu.VMEM((n_out, tiles, 2, nb, rk), BF16),
            pltpu.VMEM((n_out, groups, 2, ny, nz * rows, nb // groups), BF16),
            pltpu.VMEM((nch, ny, nz, n_out, part_rows, rk), F32),
            pltpu.VMEM((nch, ny, nz, n_out, part_rows, rk), BF16),
            pltpu.VMEM((nch, ny, nz, n_out, part_rows, rk), BF16),
            pltpu.VMEM((nch, nz, n_out, part_rows, rk), F32),
            pltpu.VMEM((nch, nz, n_out, part_rows, rk), BF16),
            pltpu.VMEM((nch, nz, n_out, part_rows, rk), BF16),
            pltpu.VMEM((nch, nz, n_out, part_rows, rk), BF16),
            pltpu.VMEM((n_out, rows, rk), F32),
            pltpu.VMEM((nch, ny, nz, n_out, part_rows, rk), BF16),
            pltpu.VMEM((n_out, cuts, nz, rows // cuts, rk), F32),
            pltpu.VMEM((n_out, cuts, ny, nz, rows // cuts, rk), BF16),
            pltpu.VMEM((n_out, cuts, ny, nz, rows // cuts, rk), BF16),
            pltpu.VMEM((n_out, cuts, nz, rows // cuts, rk), F32),
            pltpu.VMEM((n_out, cuts, nz, rows // cuts, rk), BF16),
            pltpu.VMEM((n_out, cuts, nz, rows // cuts, rk), BF16),
            pltpu.VMEM((n_out, rk, rk), F32),
            pltpu.VMEM((n_out, 1, rk), F32),
            pltpu.VMEM((n_out, rk, 3 * rk), BF16),
            pltpu.SemaphoreType.DMA((6,)),
            pltpu.SemaphoreType.DMA((n_out,)),
            pltpu.SemaphoreType.DMA((8,)),
            pltpu.SemaphoreType.DMA((1 + 2 * tpd * (nx - 1),)),
            pltpu.SemaphoreType.DMA((1 + 2 * nch * (nx - 1),)),
            pltpu.SemaphoreType.DMA((3, count)),
            pltpu.SemaphoreType.DMA((count,)),
            pltpu.SemaphoreType.DMA((2, n_out, cuts)),
        ],
        compiler_params=pltpu.CompilerParams(
            collective_id=0, has_side_effects=True, vmem_limit_bytes=60 * 1024 * 1024
        ),
    )(left_u.reshape(tpd, n_in, nch, part_rows, rk), left_v, right_u, right_v, sketch, tile_index, slot_mask)
    return both[0] * math.sqrt(nb), both[1] * 2.0


def solution(mesh):
    return jax.shard_map(
        functools.partial(body, mesh.shape["inner"], mesh.shape["cols"]),
        mesh=mesh,
        in_specs=(
            P(("inner", "cols"), None, None),
            P(("inner", "cols"), None, None),
            P("cols", "inner", None, None),
            P("cols", "inner", None, None),
            P("cols", None, None),
            P("cols", "inner"),
            P("cols", "inner"),
        ),
        out_specs=(P("cols", "inner", None), P("cols", "inner", None)),
        check_vma=False,
    )
```

```python
import functools
import math

import jax
import jax.numpy as jnp
from jax import lax
from jax.experimental import pallas as pl
from jax.experimental.pallas import tpu as pltpu
from jax.sharding import PartitionSpec as P

MESH = pl.DeviceIdType.MESH
F32 = jnp.float32
BF16 = jnp.bfloat16
NN = (((1,), (0,)), ((), ()))
NT = (((1,), (1,)), ((), ()))
TN = (((0,), (0,)), ((), ()))


def mm(a, b, dims):
    return lax.dot_general(a, b, dims, preferred_element_type=F32)


def split(a):
    hi = a.astype(BF16)
    return hi, (a - hi.astype(F32)).astype(BF16)


LEFT = (0, 0, 1, 1, 0, 2)
RIGHT = (0, 1, 0, 1, 2, 0)


def stack(a, order):
    first = a.astype(BF16).astype(F32)
    second = (a - first).astype(BF16).astype(F32)
    parts = (first, second, a - first - second)
    return jnp.concatenate([parts[i] for i in order], axis=0).astype(BF16)


def wide(parts):
    return jnp.concatenate(parts, axis=1)


def kernel(
    n_in, n_co, left_u, left_v, right_u, right_v, sketch, index_hbm, mask_hbm, outs,
    ug, vg, ru, rv, sk, skt, index, mask, inv, lv, pb, pk, mix, wt, ct,
    ybuf, sbuf, r1, s2f, s2b, r2, r3, yrow, yb,
    cbuf, csbuf, cr1, cs2f, cs2b, cr2, xm, scale, inverse,
    load_sem, rv_sem, send_sem, v_sem, u_sem, sum_sem, ag_sem, back_sem,
):
    nx = n_co // 2
    ny = nx
    nz = n_in // ny
    tpd, nb, rk = left_v.shape
    nch, part_rows = ug.shape[0], ug.shape[3]
    groups = ct.shape[1]
    cuts = cbuf.shape[1]
    tiles = tpd * n_co
    n_out, slots = right_u.shape[:2]
    rows = nb // n_in
    me_in = lax.axis_index("inner")
    me_co = lax.axis_index("cols")
    x, core = lax.div(me_co, 2), lax.rem(me_co, 2)
    z, y = lax.div(me_in, ny), lax.rem(me_in, ny)
    def co_at(dx):
        return lax.rem(x + dx, nx) * 2 + core

    def other_at(dx):
        return lax.rem(x + dx, nx) * 2 + (1 - core)

    partner = other_at(0)

    def z_at(dz):
        return lax.rem(z + dz, nz) * ny + y

    def y_at(dy):
        return z * ny + lax.rem(y + dy, ny)

    half = nz // 2
    depth = jnp.minimum(z, nz - 1 - z)
    inwards = jnp.where(z < half, 1, -1)
    inner_at = (z + inwards) * ny + y
    outer_at = (z - inwards) * ny + y

    parts = []
    for c in range(nch):
        n = n_out // 2 if c < nch - 1 else 1
        parts += [(c, j, n) for j in range(0, n_out, n)]
    V_OUT, U_OUT, SUM_Y, SUM_Z, GATHER_Z, GATHER_Y, BACK_Y, BACK_Z = range(8)

    def remote(src, dst, kind, r_sem, **dev):
        return pltpu.make_async_remote_copy(
            src_ref=src, dst_ref=dst, send_sem=send_sem.at[kind], recv_sem=r_sem,
            device_id=dev, device_id_type=MESH,
        )

    def arrived(part, r_sem):
        pltpu.make_async_copy(part, part, r_sem).wait()

    own = pl.ds(me_co * tpd, tpd)
    tables = [pltpu.make_async_copy(index_hbm, index, load_sem.at[0]), pltpu.make_async_copy(mask_hbm, mask, load_sem.at[1])]
    first_sketch = pltpu.make_async_copy(sketch, sk, load_sem.at[2])
    rv_load = [pltpu.make_async_copy(right_v.at[j], rv.at[j], rv_sem.at[j]) for j in range(n_out)]
    own_v = pltpu.make_async_copy(left_v, vg.at[own], load_sem.at[3])
    ru_load = pltpu.make_async_copy(right_u, ru, load_sem.at[4])
    for copy in tables + [first_sketch] + rv_load[:2]:
        copy.start()

    barrier = pltpu.get_barrier_semaphore()
    for dx in range(1, nx):
        pl.semaphore_signal(barrier, inc=1, device_id={"cols": co_at(dx)}, device_id_type=MESH)
    pl.semaphore_signal(barrier, inc=1, device_id={"cols": partner}, device_id_type=MESH)
    for dy in range(1, ny):
        pl.semaphore_signal(barrier, inc=1, device_id={"inner": y_at(dy)}, device_id_type=MESH)
    for dz in range(1, nz):
        pl.semaphore_signal(barrier, inc=1, device_id={"inner": z_at(dz)}, device_id_type=MESH)
    pl.semaphore_wait(barrier, nx - 1 + 1 + ny - 1 + nz - 1)

    for i in range(tpd):
        for dx in range(1, nx):
            remote(left_v.at[i], vg.at[me_co * tpd + i], V_OUT, v_sem.at[1 + 2 * ((dx - 1) * tpd + i)], cols=co_at(dx)).start()
    for c in range(nch):
        for dx in range(1, nx):
            remote(left_u.at[:, :, c], ug.at[c, own], U_OUT, u_sem.at[1 + 2 * ((dx - 1) * nch + c)], cols=co_at(dx)).start()
    for copy in rv_load[2:] + [own_v]:
        copy.start()
    remote(left_v, vg.at[own], V_OUT, v_sem.at[0], cols=partner).start()
    ru_load.start()
    for c in range(nch):
        pltpu.make_async_copy(left_u.at[:, :, c], ug.at[c, own], load_sem.at[5]).start()
    for c in range(nch):
        remote(left_u.at[:, :, c], ug.at[c, own], U_OUT, u_sem.at[0], cols=partner).start()

    for copy in tables:
        copy.wait()
    for j in range(n_out):
        named = [lax.rem(index[j, s], tiles) for s in range(slots)]
        alive = [mask[j, s] for s in range(slots)]
        for k in range(tiles):
            at, live = jnp.int32(0), jnp.int32(0)
            for s in range(slots):
                hit = named[s] == k
                at = jnp.where(hit, s, at)
                live = jnp.where(hit, alive[s], live)
            inv[j, k] = at
            lv[j, k] = live

    first_sketch.wait()

    @pl.loop(0, n_out)
    def _(j):
        skt[...] = jnp.transpose(sk[j])
        pltpu.make_async_copy(right_v.at[j], rv.at[j], rv_sem.at[j]).wait()
        for s in range(0, slots, 2):
            out = mm(skt[...], wide([rv[j, s], rv[j, s + 1]]), NN)
            for i in range(2):
                hi, lo = split(out[:, i * rk : (i + 1) * rk])
                pb[j, s + i, :rk] = hi
                pb[j, s + i, rk:] = lo

    own_v.wait()
    ru_load.wait()

    def pair(k):
        vt = jnp.transpose(vg[k])
        for first in range(0, n_out, 2):
            js = (first, first + 1)
            at = [inv[j, k] for j in js]
            out = mm(vt, wide([ru[j, s] for j, s in zip(js, at)]), NN)
            for i, (j, s) in enumerate(zip(js, at)):
                hi, lo = split(out[:, i * rk : (i + 1) * rk] * lv[j, k].astype(F32))
                both = wide([hi, lo])
                pk[j, k] = both
                probe = pb[j, s]
                mixed = mm(both, wide([probe, probe]), NT)
                mix[k, :, j * rk : (j + 1) * rk] = (mixed[:, :rk] + mixed[:, rk:]).astype(BF16)

    def fold_one(k):
        for j in range(n_out):
            right = rv[j, inv[j, k]]
            wt[j, k, 0], wt[j, k, 1] = split(mm(wide([right, right]), pk[j, k], NT))

    folds = []

    def fold(n):
        todo = [folds.pop(0) for _ in range(min(n, len(folds)))]
        for k in todo:
            fold_one(k)

    for i in range(tpd):
        k = me_co * tpd + i
        pair(k)
        folds.append(k)
    arrived(vg.at[pl.ds(partner * tpd, tpd)], v_sem.at[0])
    for i in range(tpd):
        k = partner * tpd + i
        pair(k)
        folds.append(k)

    for i in range(tpd):
        for dx in range(1, nx):
            k = co_at(nx - dx) * tpd + i
            arrived(vg.at[k], v_sem.at[1 + 2 * ((dx - 1) * tpd + i)])
            remote(vg.at[k], vg.at[k], V_OUT, v_sem.at[2 + 2 * ((dx - 1) * tpd + i)], cols=partner).start()
        for dx in range(1, nx):
            k = co_at(nx - dx) * tpd + i
            pair(k)
            folds.append(k)
        fold(1)
        for dx in range(1, nx):
            k = other_at(nx - dx) * tpd + i
            arrived(vg.at[k], v_sem.at[2 + 2 * ((dx - 1) * tpd + i)])
        for dx in range(1, nx):
            k = other_at(nx - dx) * tpd + i
            pair(k)
            folds.append(k)
        if i < tpd - 1:
            fold(1)
    pltpu.make_async_copy(left_v, vg.at[own], load_sem.at[5]).wait()
    arrived(vg.at[own], u_sem.at[0])

    def block_u(c, position):
        return ug.at[c, pl.ds(position * tpd, tpd)]

    def chunk_u(c):
        return wide([ug[c, k].reshape(nb // nch, rk) for k in range(tiles)])

    def sketched(c):
        total = mm(chunk_u(c), mix[...].reshape(tiles * rk, n_out * rk), NN)
        low = total.astype(BF16)
        for j in range(n_out):
            at = slice(j * rk, (j + 1) * rk)
            shape = (nz, ny, part_rows, rk)
            full = total[:, at].reshape(shape)
            part = low[:, at].reshape(shape)
            for yy in range(ny):
                ybuf[c, yy, :, j] = full[:, yy]
                sbuf[c, yy, :, j] = part[:, yy]
        for q, (of, first, n) in enumerate(parts):
            if of == c:
                at = pl.ds(first, n)
                for dy in range(1, ny):
                    remote(
                        sbuf.at[c, lax.rem(y + dy, ny), :, at], r1.at[c, dy, :, at],
                        SUM_Y, sum_sem.at[0, q], inner=y_at(dy),
                    ).start()

    def second(q):
        c, first, n = parts[q]
        at = pl.ds(first, n)
        arrived(r1.at[c, pl.ds(1, ny - 1), :, at], sum_sem.at[0, q])
        total = ybuf[c, y, :, at]
        for dy in range(1, ny):
            total = total + r1[c, dy, :, at].astype(F32)
        s2f[c, :, at] = total
        if half > 1:
            @pl.when(depth == 0)
            def _():
                s2b[c, :, at] = total.astype(BF16)
                remote(s2b.at[c, :, at], r2.at[c, :, at], SUM_Z, sum_sem.at[1, q], inner=inner_at).start()

    def third(q, level):
        c, first, n = parts[q]
        at = pl.ds(first, n)

        @pl.when(depth == level)
        def _():
            arrived(r2.at[c, :, at], sum_sem.at[1, q])
            total = s2f[c, :, at] + r2[c, :, at].astype(F32)
            s2b[c, :, at] = total.astype(BF16)
            land, sem = (r2, 1) if level < half - 1 else (r3, 2)
            remote(s2b.at[c, :, at], land.at[c, :, at], SUM_Z, sum_sem.at[sem, q], inner=inner_at).start()
            s2f[c, :, at] = total

    def to_y(q):
        c, first, n = parts[q]
        part = yb.at[c, y, :, pl.ds(first, n)]
        for dy in range(1, ny):
            remote(part, part, GATHER_Y, ag_sem.at[q], inner=y_at(dy)).start()

    def to_outer(q):
        c, first, n = parts[q]
        part = yb.at[c, y, :, pl.ds(first, n)]
        remote(part, part, GATHER_Z, sum_sem.at[1, q], inner=outer_at).start()

    def last(q):
        c, first, n = parts[q]
        at = pl.ds(first, n)

        @pl.when(depth == half - 1)
        def _():
            arrived(r3.at[c, :, at], sum_sem.at[2, q])
            total = s2f[c, :, at] + r3[c, :, at].astype(F32)
            yb[c, y, :, at] = total.astype(BF16)
            if half > 1:
                to_outer(q)
            to_y(q)
            s2f[c, :, at] = total
            yrow[at, c * part_rows : (c + 1) * part_rows] = s2f[c, z, at]

    def spread(q, level):
        c, first, n = parts[q]
        at = pl.ds(first, n)

        @pl.when(depth == level)
        def _():
            arrived(yb.at[c, y, :, at], sum_sem.at[1, q])
            if level > 0:
                to_outer(q)
            to_y(q)
            yrow[at, c * part_rows : (c + 1) * part_rows] = yb[c, y, z, at].astype(F32)

    def complete(q):
        c, first, n = parts[q]
        arrived(yb.at[c, pl.ds(0, ny - 1), :, pl.ds(first, n)], ag_sem.at[q])

    span = nch // groups

    def tile_t(j, g):
        left = wide([wt[j, k, h] for h in range(2) for k in range(tiles)])
        right = jnp.concatenate([chunk_u(g * span + i) for i in range(span)], axis=0)
        for h, part in enumerate(split(mm(left, wide([right, right]), NT))):
            part = part.reshape(nz, ny, rows, nb // groups)
            for yy in range(ny):
                ct[j, g, h, yy] = part[:, yy].reshape(nz * rows, nb // groups)

    def y_chunk(c, j):
        return jnp.concatenate([yb[c, yy, zz, j] for zz in range(nz) for yy in range(ny)], axis=0)

    def y_of(j):
        return jnp.concatenate([y_chunk(c, j) for c in range(nch)], axis=0)

    def back(j):
        right = y_of(j)
        right = jnp.concatenate([right, right], axis=0)

        def share(yy):
            left = wide([ct[j, g, h, yy] for h in range(2) for g in range(groups)])
            return mm(left, right, NN).reshape(nz, cuts, rows // cuts, rk)

        for dy in range(1, ny):
            part = share(lax.rem(y + dy, ny)).astype(BF16)
            for p in range(cuts):
                csbuf[j, p, dy] = part[:, p]
                remote(
                    csbuf.at[j, p, dy], cr1.at[j, p, dy], BACK_Y, back_sem.at[0, j, p], inner=y_at(dy)
                ).start()
        part = share(y)
        for p in range(cuts):
            cbuf[j, p] = part[:, p]

    def back_second(j, p):
        total = cbuf[j, p]
        arrived(cr1.at[j, p, pl.ds(1, ny - 1)], back_sem.at[0, j, p])
        for dy in range(1, ny):
            total = total + cr1[j, p, dy].astype(F32)
        cs2f[j, p] = total
        cs2b[j, p] = total.astype(BF16)
        for dz in range(1, nz):
            remote(
                cs2b.at[j, p, lax.rem(z + dz, nz)], cr2.at[j, p, dz], BACK_Z, back_sem.at[1, j, p], inner=z_at(dz)
            ).start()

    def back_last(j):
        parts = []
        for p in range(cuts):
            total = cs2f[j, p, z]
            arrived(cr2.at[j, p, pl.ds(1, nz - 1)], back_sem.at[1, j, p])
            for dz in range(1, nz):
                total = total + cr2[j, p, dz].astype(F32)
            parts.append(total)
        return jnp.concatenate(parts, axis=0)

    work = [(j, g) for g in range(groups) for j in range(n_out)]

    def pass_on_u(c):
        for dx in range(1, nx):
            part = block_u(c, co_at(nx - dx))
            arrived(part, u_sem.at[1 + 2 * ((dx - 1) * nch + c)])
            remote(part, part, U_OUT, u_sem.at[2 + 2 * ((dx - 1) * nch + c)], cols=partner).start()

    def gram(c):
        for j in range(n_out):
            part = y_chunk(c, j)
            total = mm(part, part, TN)
            xm[j] = total if c == 0 else xm[j] + total

    pass_on_u(0)
    for c in range(nch):
        if c == 0:
            fold(1)
        if c < nch - 1:
            pass_on_u(c + 1)
        if c == nch - 1:
            fold(2)
        for dx in range(1, nx):
            arrived(block_u(c, other_at(nx - dx)), u_sem.at[2 + 2 * ((dx - 1) * nch + c)])
        sketched(c)
        if c == 1:
            fold(1)

    count = len(parts)
    stages = [second]
    stages += [functools.partial(third, level=i) for i in range(1, half)]
    stages += [last]
    stages += [functools.partial(spread, level=i) for i in range(half - 2, -1, -1)]
    times = {}
    for q, (c, first, n) in enumerate(parts):
        start = 1.4 * (c + 0.7 * first / n_out)
        for i in range(len(stages)):
            times[i, q] = start + (0.0, *[3.1 + 3.6 * h for h in range(half)], *[2.4 * (h + 1) + 3.6 * half - 0.5 for h in range(half - 1)])[i]
    order = sorted(times, key=times.get)
    def products(here):
        @pl.when(here)
        def _():
            for j, g in work:
                tile_t(j, g)

    for i, q in order:
        stages[i](q)
        if (i, q) == (0, 1):
            fold(len(folds))
        if (i, q) == (0, count - 1):
            products(depth < half - 1)
        if (i, q) == (half, count - 1):
            products(depth == half - 1)
    for c in range(nch):
        for q in range(count):
            if parts[q][0] == c:
                complete(q)
                if c == nch - 1:
                    back(parts[q][1])
        if c < nch - 1:
            gram(c)
    gram(nch - 1)
    row_id = lax.broadcasted_iota(jnp.int32, (rk, rk), 0)
    col_id = lax.broadcasted_iota(jnp.int32, (rk, rk), 1)
    for j in range(n_out):
        whole = xm[j]
        diag = jnp.where(row_id == col_id, whole, 0.0)
        s_row = lax.rsqrt(jnp.sum(diag, axis=0, keepdims=True))
        s_col = lax.rsqrt(jnp.sum(diag, axis=1, keepdims=True))
        scale[j] = s_row
        xm[j] = whole * s_col * s_row

    sub8 = lax.broadcasted_iota(jnp.int32, (8, rk), 0)
    lane8 = lax.broadcasted_iota(jnp.int32, (8, rk), 1)

    def eliminate(start, stop):
        @pl.loop(start, stop)
        def _(b):
            eliminate_block(b)

    def eliminate_block(b):
        base = b * 8 if isinstance(b, int) else pl.multiple_of(b * 8, 8)
        near = lane8 - base
        at = pl.ds(base, 8)
        slabs = [xm[j, at] for j in range(n_out)]
        cols = [
            [
                jnp.broadcast_to(jnp.sum(jnp.where(near == i, slab, 0.0), axis=1, keepdims=True), (8, rk))
                for i in range(8)
            ]
            for slab in slabs
        ]
        pivots = [jnp.ones((8, rk), F32)] * n_out
        for k in range(8):
            hot = jnp.where(near[:1] == k, 1.0, 0.0)
            for j in range(n_out):
                column = cols[j][k]
                pivots[j] = jnp.where(sub8 == k, column[k : k + 1], pivots[j])
                weight = jnp.where(sub8 > k, column * (1.0 / column[k : k + 1]), 0.0)
                slabs[j] = slabs[j] - weight * (slabs[j][k : k + 1] + hot)
                for i in range(k + 1, 8):
                    cols[j][i] = cols[j][i] - weight * cols[j][i][k : k + 1]
        for j in range(n_out):
            ahead = jnp.where(near >= 8, slabs[j] / pivots[j], 0.0)
            unit = jnp.where(near == sub8, 1.0, jnp.where((near >= 0) & (near > sub8) & (near < 8), 0.0, slabs[j]))
            near_all = col_id - base
            clear = (row_id - base >= 8) & (near_all >= 0) & (near_all < 8)
            xm[j] = jnp.where(clear, 0.0, xm[j]) - mm(stack(ahead, LEFT), stack(unit, RIGHT), TN)
            xm[j, at] = slabs[j]

    blocks = rk // 8
    pieces = [(j, p) for j in range(n_out) for p in range(cuts)]
    done = 0
    for n, (j, p) in enumerate(pieces):
        upto = blocks * (2 * len(pieces) + 10 * n) // (16 * len(pieces))
        if upto > done:
            eliminate(done, upto)
            done = upto
        back_second(j, p)
    eliminate(done, blocks)

    for j in range(n_out):
        left = xm[j]
        pivots = jnp.sum(jnp.where(row_id == col_id, left, 0.0), axis=1, keepdims=True)
        lower = jnp.where(col_id < row_id, left, jnp.where(row_id == col_id, 1.0, 0.0))
        hi, lo = split(lower * lax.rsqrt(pivots) * scale[j])
        inverse[j] = wide([hi, lo, hi])
        hi, lo = split(yrow[j])
        outs[0, j] = mm(wide([hi, hi, lo]), inverse[j], NT)
    for j in range(n_out):
        hi, lo = split(back_last(j) * 0.5)
        outs[1, j] = mm(wide([hi, hi, lo]), inverse[j], NT)

    def gone(ref, kind):
        pltpu.make_async_copy(ref, ref, send_sem.at[kind]).wait()

    gone(vg.at[pl.ds(0, tiles - tpd)], V_OUT)
    gone(vg.at[pl.ds(0, tiles - tpd)], U_OUT)
    gone(r1.at[:, pl.ds(1, ny - 1)], SUM_Y)
    gone(s2b, SUM_Z)
    if half > 1:
        @pl.when(depth > 0)
        def _():
            gone(yb.at[:, 0], GATHER_Z)
    gone(yb.at[:, pl.ds(0, ny - 1)], GATHER_Y)
    gone(cr1.at[:, :, pl.ds(1, ny - 1)], BACK_Y)
    gone(cr2.at[:, :, pl.ds(1, nz - 1)], BACK_Z)


def body(n_in, n_co, left_u, left_v, right_u, right_v, sketch, tile_index, slot_mask):
    n_out, slots, nb, rk = right_u.shape
    tpd = left_u.shape[0]
    tiles = tpd * n_co
    nx = n_co // 2
    ny = nx
    nz = n_in // ny
    rows = nb // n_in
    nch = rows // 16
    part_rows = rows // nch
    groups = max(1, nch // 2)
    count = 2 * (nch - 1) + n_out
    cuts = 2 if rows % 32 == 0 else 1
    both = pl.pallas_call(
        functools.partial(kernel, n_in, n_co),
        out_shape=jax.ShapeDtypeStruct((2, n_out, rows, rk), F32),
        in_specs=[pl.BlockSpec(memory_space=pl.ANY)] * 7,
        out_specs=pl.BlockSpec(memory_space=pltpu.VMEM),
        scratch_shapes=[
            pltpu.VMEM((nch, tiles, n_in, part_rows, rk), BF16),
            pltpu.VMEM((tiles, nb, rk), BF16),
            pltpu.VMEM((n_out, slots, nb, rk), BF16),
            pltpu.VMEM((n_out, slots, nb, rk), BF16),
            pltpu.VMEM((n_out, nb, rk), BF16),
            pltpu.VMEM((rk, nb), BF16),
            pltpu.SMEM((n_out, slots), jnp.int32),
            pltpu.SMEM((n_out, slots), jnp.int32),
            pltpu.SMEM((n_out, tiles), jnp.int32),
            pltpu.SMEM((n_out, tiles), jnp.int32),
            pltpu.VMEM((n_out, slots, 2 * rk, rk), BF16),
            pltpu.VMEM((n_out, tiles, rk, 2 * rk), BF16),
            pltpu.VMEM((tiles, rk, n_out * rk), BF16),
            pltpu.VMEM((n_out, tiles, 2, nb, rk), BF16),
            pltpu.VMEM((n_out, groups, 2, ny, nz * rows, nb // groups), BF16),
            pltpu.VMEM((nch, ny, nz, n_out, part_rows, rk), F32),
            pltpu.VMEM((nch, ny, nz, n_out, part_rows, rk), BF16),
            pltpu.VMEM((nch, ny, nz, n_out, part_rows, rk), BF16),
            pltpu.VMEM((nch, nz, n_out, part_rows, rk), F32),
            pltpu.VMEM((nch, nz, n_out, part_rows, rk), BF16),
            pltpu.VMEM((nch, nz, n_out, part_rows, rk), BF16),
            pltpu.VMEM((nch, nz, n_out, part_rows, rk), BF16),
            pltpu.VMEM((n_out, rows, rk), F32),
            pltpu.VMEM((nch, ny, nz, n_out, part_rows, rk), BF16),
            pltpu.VMEM((n_out, cuts, nz, rows // cuts, rk), F32),
            pltpu.VMEM((n_out, cuts, ny, nz, rows // cuts, rk), BF16),
            pltpu.VMEM((n_out, cuts, ny, nz, rows // cuts, rk), BF16),
            pltpu.VMEM((n_out, cuts, nz, rows // cuts, rk), F32),
            pltpu.VMEM((n_out, cuts, nz, rows // cuts, rk), BF16),
            pltpu.VMEM((n_out, cuts, nz, rows // cuts, rk), BF16),
            pltpu.VMEM((n_out, rk, rk), F32),
            pltpu.VMEM((n_out, 1, rk), F32),
            pltpu.VMEM((n_out, rk, 3 * rk), BF16),
            pltpu.SemaphoreType.DMA((6,)),
            pltpu.SemaphoreType.DMA((n_out,)),
            pltpu.SemaphoreType.DMA((8,)),
            pltpu.SemaphoreType.DMA((1 + 2 * tpd * (nx - 1),)),
            pltpu.SemaphoreType.DMA((1 + 2 * nch * (nx - 1),)),
            pltpu.SemaphoreType.DMA((3, count)),
            pltpu.SemaphoreType.DMA((count,)),
            pltpu.SemaphoreType.DMA((2, n_out, cuts)),
        ],
        compiler_params=pltpu.CompilerParams(
            collective_id=0, has_side_effects=True, vmem_limit_bytes=52 * 1024 * 1024
        ),
    )(*[
        pltpu.with_memory_space_constraint(a, pltpu.HBM)
        for a in (
            left_u.reshape(tpd, n_in, nch, part_rows, rk), left_v, right_u, right_v, sketch, tile_index, slot_mask
        )
    ])
    return both[0] * math.sqrt(nb), both[1] * 2.0


def solution(mesh):
    return jax.shard_map(
        functools.partial(body, mesh.shape["inner"], mesh.shape["cols"]),
        mesh=mesh,
        in_specs=(
            P(("inner", "cols"), None, None),
            P(("inner", "cols"), None, None),
            P("cols", "inner", None, None),
            P("cols", "inner", None, None),
            P("cols", None, None),
            P("cols", "inner"),
            P("cols", "inner"),
        ),
        out_specs=(P("cols", "inner", None), P("cols", "inner", None)),
        check_vma=False,
    )
```
